32 devices in a mesh: fsdp: 4 (over z), adapter: 8 (over y, x, core).
Axes of the slice: x: 2, y: 2, z: 4, core: 2. Of those that a mesh axis runs over, the one named last changes fastest.
Arguments:
- tokens: bfloat16 [2048, 8192], P('adapter', 'fsdp'), may hold values from -6 to 6
- tenant: int32 [2048], P('adapter'), may hold values from 0 to 63, as said below
- send_list: int32 [8, 8, 128], P('adapter'), may hold values from -1 to 255, as said below
- base_weight: bfloat16 [8192, 2048], P('fsdp'), may hold values from -0.09375 to 0.09375
- down_weight: bfloat16 [64, 8192, 128], P('adapter', 'fsdp'), may hold values from -0.0625 to 0.0625
- up_projection_weight: bfloat16 [64, 64, 2048], P('adapter', None, 'fsdp'), may hold values from -0.75 to 0.75
- cotangent: bfloat16 [2048, 2048], P('adapter', 'fsdp'), may hold values from -3 to 3
Outputs:
- projected: bfloat16 [2048, 2048], P('adapter', 'fsdp')
- token_gradient: bfloat16 [2048, 8192], P('adapter', 'fsdp')
- down_weight_gradient: bfloat16 [64, 8192, 128], P('adapter', 'fsdp')
- up_weight_gradient: bfloat16 [64, 64, 2048], P('adapter', None, 'fsdp')
The draws below stay inside these ranges and needn't reach their ends.
Inputs may be any that keep to these rules, and one draw needn't show every extreme that they name: `tenant`: adapter t belongs to owner t // 8. Among the 256 rows of one index of adapter at most 128 belong to the adapters of one owner, and one owner, the same for every index, has exactly 128 of them. send_list[i, o, :] lists in increasing order the rows (numbered within the 256 rows of index i of adapter) whose tenant belongs to owner o, then -1 in the slots left; every row stands in exactly one list.
All inputs are finite; a program needn't handle non-finite values.
Results may differ from the reference program's by a relative error of at most 0.005.
Values may be sent and summed in bfloat16 or wider, within the bound.
No kernel may reach another device: no remote copies, remote signals or barrier semaphores. Data moves between devices by JAX's collectives and lax.ppermute only.
A program may use at most 128 MiB of HBM per device.

```python
import jax
import jax.numpy as jnp
from jax import lax

D = 8192
KV = 1024
RANK = 64
ADP_DEV = 8
TOK_GRP = 256
ADAPTERS = 64
TOKENS = 2048
CAP = 128
N_ADAPTER = 8


def owner_tables(key):
    groups = TOKENS // TOK_GRP
    holder_list = ADAPTERS // ADP_DEV
    base_key = jax.random.fold_in(key, 4242)
    hot_owner = jax.random.randint(jax.random.fold_in(base_key, 1), (), 0, holder_list).astype(jnp.int32)
    group_keys = jax.random.split(jax.random.fold_in(base_key, 2), groups)

    def one_group(group_key):
        perm_key, shuffle_key = jax.random.split(group_key)
        free_slots = jax.random.permutation(perm_key, (holder_list - 1) * CAP)[:TOK_GRP - CAP]
        other_owner = (free_slots // CAP).astype(jnp.int32)
        other_owner = other_owner + (other_owner >= hot_owner).astype(jnp.int32)
        owner_rows = jnp.concatenate([jnp.full((CAP,), hot_owner, jnp.int32), other_owner])
        return jax.random.permutation(shuffle_key, owner_rows).astype(jnp.int32)
    owner_rows = jax.vmap(one_group)(group_keys)
    local_ids = jax.random.randint(jax.random.fold_in(base_key, 3), (groups, TOK_GRP), 0, ADP_DEV).astype(jnp.int32)
    return (owner_rows, local_ids)


def draw_tenant(key, part):
    owner_rows, local_ids = owner_tables(key)
    return (owner_rows * ADP_DEV + local_ids).reshape(TOKENS).astype(jnp.int32)


def draw_send_list(key, part):
    owner_rows, local_ids = owner_tables(key)
    holder_list = ADAPTERS // ADP_DEV
    row_ids = jnp.arange(TOK_GRP, dtype=jnp.int32)
    owner_ids = jnp.arange(holder_list, dtype=jnp.int32)
    slot_ids = jnp.arange(CAP, dtype=jnp.int32)

    def one_group(row_owner):
        sort_keys = row_owner * TOK_GRP + row_ids
        sorted_rows = jnp.argsort(sort_keys, stable=True).astype(jnp.int32)
        counts = jnp.sum((row_owner[None, :] == owner_ids[:, None]).astype(jnp.int32), axis=1)
        starts = jnp.cumsum(counts) - counts
        slot_pos = jnp.clip(starts[:, None] + slot_ids[None, :], 0, TOK_GRP - 1)
        return jnp.where(slot_ids[None, :] < counts[:, None], sorted_rows[slot_pos], -1).astype(jnp.int32)
    return jax.vmap(one_group)(owner_rows)


def with_spikes(entries, stream_key, source, target, parts, factor):
    owner, partner = [(jnp.arange(entries.shape[position]) // (entries.shape[position] // parts)).reshape([-1 if axis == position else 1 for axis in range(entries.ndim)]) for position in (source, target)]
    chosen = jax.random.permutation(stream_key, parts)[partner]
    strong = (owner == chosen) | (owner == (partner + parts // 2) % parts)
    return jnp.where(strong, factor * entries, entries)


def levels(rng, extent, cuts, least, high):
    level, own = 1.0, jax.random.fold_in(rng, 6)
    for dim, shards_of in cuts:
        steps = jnp.exp(jax.random.uniform(jax.random.fold_in(own, dim), (shards_of,), jnp.float32, least / len(cuts), high / len(cuts)))
        level = level * jnp.repeat(steps, extent[dim] // shards_of).reshape([-1 if axis == dim else 1 for axis in range(len(extent))])
    return level


def normal_values(key, shape, deviation, most, cuts=(), kind=jnp.bfloat16):
    entries = deviation * jax.random.normal(key, shape, jnp.float32)
    if cuts:
        entries = entries * levels(key, shape, cuts, -0.22, 0.18)
    return jnp.clip(entries, -most, most).astype(kind)


def heavy_noise(own_key, dims, scale, most, cuts, heavy, kind=jnp.bfloat16):
    array = scale * jax.random.normal(own_key, dims, jnp.float32)
    if cuts:
        array = array * levels(own_key, dims, cuts, -0.22, 0.18)
    return jnp.clip(with_spikes(array, jax.random.fold_in(own_key, 3), *heavy), -most, most).astype(kind)


def setup_inputs(seed: int = 0) -> dict:
    seeds = jax.random.split(jax.random.key(seed), 8)
    return {
        "tokens": normal_values(seeds[0], (TOKENS, D), 1.0, 6.0, ((0, 8), (1, 4))),
        "tenant": draw_tenant(jax.random.fold_in(seeds[7], 71), 0),
        "send_list": draw_send_list(jax.random.fold_in(seeds[7], 71), 0),
        "base_weight": heavy_noise(seeds[3], (D, 2 * KV), D ** -0.5, 0.09375, ((0, 4),), (0, 1, 4, 2.0)),
        "down_weight": normal_values(seeds[4], (ADAPTERS, D, 2 * RANK), D ** -0.5, 0.0625, ((0, 8), (1, 4))),
        "up_projection_weight": normal_values(seeds[5], (ADAPTERS, RANK, 2 * KV), RANK ** -0.5, 0.75, ((0, 8), (2, 4))),
        "cotangent": normal_values(seeds[6], (TOKENS, 2 * KV), 0.5, 3.0, ((0, 8), (1, 4))),
    }


adapter_scale = 0.5


def rounded(values):
    return lax.optimization_barrier(values.astype(jnp.bfloat16)).astype(jnp.float32)


def reference(tokens, tenant, send_list, base_weight, down_weight, up_projection_weight, cotangent):
    groups = N_ADAPTER
    slot_total = N_ADAPTER * CAP
    base_out = jnp.dot(tokens, base_weight, preferred_element_type=jnp.float32)
    input_frozen_part = jnp.dot(cotangent, base_weight.T, preferred_element_type=jnp.float32)
    tokens_grp = tokens.reshape(groups, TOK_GRP, D)
    grads_grp = cotangent.reshape(groups, TOK_GRP, 2 * KV)
    local_ids = (tenant % ADP_DEV).reshape(groups, TOK_GRP)
    group_ids = jnp.arange(groups, dtype=jnp.int32)[:, None]
    adapter_ids = jnp.arange(ADP_DEV, dtype=jnp.int32)

    def per_owner(totals, owner_idx):
        projection_accumulator, back_acc = totals
        listed = send_list[:, owner_idx, :]
        present = listed >= 0
        safe_rows = jnp.where(present, listed, 0)
        input_rows = tokens_grp[group_ids, safe_rows].reshape(slot_total, D).astype(jnp.float32)
        rows_dy = grads_grp[group_ids, safe_rows].reshape(slot_total, 2 * KV).astype(jnp.float32)
        picked = local_ids[group_ids, safe_rows].reshape(slot_total)
        weight_table = ((picked[:, None] == adapter_ids[None, :]) & present.reshape(slot_total)[:, None]).astype(jnp.float32)
        holder_down_weight = lax.dynamic_slice_in_dim(down_weight, owner_idx * ADP_DEV, ADP_DEV, 0).astype(jnp.float32)
        own_up = lax.dynamic_slice_in_dim(up_projection_weight, owner_idx * ADP_DEV, ADP_DEV, 0).astype(jnp.float32)
        low_all = jnp.einsum("sd,ldk->slk", input_rows, holder_down_weight)
        low_rank = rounded(jnp.sum(low_all * weight_table[:, :, None], axis=1))
        spread_k = low_rank[:, None, :RANK] * weight_table[:, :, None]
        spread_v = low_rank[:, None, RANK:] * weight_table[:, :, None]
        key_update = jnp.einsum("slr,lrc->sc", spread_k, own_up[:, :, :KV])
        value_update = jnp.einsum("slr,lrc->sc", spread_v, own_up[:, :, KV:])
        adapter_update = (adapter_scale * jnp.concatenate([key_update, value_update], axis=1)).astype(jnp.bfloat16)
        back_k = jnp.sum(jnp.einsum("sc,lrc->slr", rows_dy[:, :KV], own_up[:, :, :KV]) * weight_table[:, :, None], axis=1)
        back_v = jnp.sum(jnp.einsum("sc,lrc->slr", rows_dy[:, KV:], own_up[:, :, KV:]) * weight_table[:, :, None], axis=1)
        back_low = rounded(jnp.concatenate([back_k, back_v], axis=1))
        widened_rows = back_low[:, None, :] * weight_table[:, :, None]
        backward_update = (adapter_scale * jnp.einsum("wnr,nyr->wy", widened_rows, holder_down_weight)).astype(jnp.bfloat16)
        down_portion = (adapter_scale * jnp.einsum("wq,wmu->mqu", input_rows, widened_rows)).astype(jnp.bfloat16)
        key_up_weight = jnp.einsum("slr,sc->lrc", spread_k, rows_dy[:, :KV])
        value_up_weight = jnp.einsum("slr,sc->lrc", spread_v, rows_dy[:, KV:])
        up_portion = (adapter_scale * jnp.concatenate([key_up_weight, value_up_weight], axis=2)).astype(jnp.bfloat16)
        destination_index = jnp.where(present, group_ids * TOK_GRP + listed, TOKENS).reshape(slot_total).astype(jnp.int32)
        projection_accumulator = projection_accumulator.at[destination_index].add(adapter_update, mode="drop")
        back_acc = back_acc.at[destination_index].add(backward_update, mode="drop")
        return (projection_accumulator, back_acc), (down_portion, up_portion)

    start_acc = (jnp.zeros((TOKENS, 2 * KV), jnp.bfloat16), jnp.zeros((TOKENS, D), jnp.bfloat16))
    (projection_accumulator, back_acc), (down_all, up_all) = lax.scan(per_owner, start_acc, jnp.arange(N_ADAPTER, dtype=jnp.int32))
    projected = (base_out + projection_accumulator.astype(jnp.float32)).astype(jnp.bfloat16)
    token_gradient = (input_frozen_part + back_acc.astype(jnp.float32)).astype(jnp.bfloat16)
    return (projected, token_gradient, down_all.reshape(ADAPTERS, D, 2 * RANK), up_all.reshape(ADAPTERS, RANK, 2 * KV))
```

```python
import jax
import jax.numpy as jnp
from jax import lax
from jax.experimental import pallas as pl
from jax.experimental.pallas import tpu as pltpu
from jax.sharding import PartitionSpec as P

KV = 1024


adapter_scale = 0.5


def down_partial(input_rows, weights_f, down_weight):
    low_all = jnp.einsum("sd,ldk->slk", input_rows, down_weight, preferred_element_type=jnp.float32)
    return jnp.sum(low_all * weights_f[:, :, None], axis=1)


def grad_partial(rows_dy, weights_f, up_projection_weight, selected_half):
    rank_size = up_projection_weight.shape[1]
    back_all = jnp.einsum(
        "sc,lrc->slr", rows_dy, up_projection_weight, preferred_element_type=jnp.float32
    )
    half_sum = jnp.sum(back_all * weights_f[:, :, None], axis=1)
    placed = jnp.zeros((rows_dy.shape[0], 2 * rank_size), jnp.float32)
    zero_idx = jnp.zeros((), jnp.int32)
    return lax.dynamic_update_slice(placed, half_sum, (zero_idx, selected_half * rank_size))


def forward_holder(low_rank, weight_table, up_projection_weight, selected_half):
    rank_size = up_projection_weight.shape[1]
    low_half = lax.dynamic_slice_in_dim(low_rank, selected_half * rank_size, rank_size, 1)
    broadcast_rows = low_half[:, None, :] * weight_table[:, :, None]
    adapter_update = adapter_scale * jnp.einsum(
        "slr,lrc->sc", broadcast_rows, up_projection_weight, preferred_element_type=jnp.float32
    )
    return (adapter_update.astype(jnp.bfloat16), broadcast_rows)


def backward_owner(back_low, weight_table, input_rows, rows_dy, broadcast_rows, down_weight):
    widened_rows = back_low[:, None, :] * weight_table[:, :, None]
    backward_update = adapter_scale * jnp.einsum(
        "wnr,nyr->wy", widened_rows, down_weight, preferred_element_type=jnp.float32
    )
    down_weight_gradient = adapter_scale * jnp.einsum(
        "wq,wmu->mqu", input_rows, widened_rows, preferred_element_type=jnp.float32
    )
    up_weight_gradient = adapter_scale * jnp.einsum(
        "slr,sc->lrc", broadcast_rows, rows_dy, preferred_element_type=jnp.float32
    )
    return (
        backward_update.astype(jnp.bfloat16),
        down_weight_gradient.astype(jnp.bfloat16),
        up_weight_gradient.astype(jnp.bfloat16),
    )


def shards_any(tokens, tenant, send_list, base_weight, down_weight, up_projection_weight, cotangent):
    rows_here = tokens.shape[0]
    width_here = tokens.shape[1]
    column_span = cotangent.shape[1]
    adapters_here = down_weight.shape[0]
    holder_list = send_list.shape[1]
    slot_capacity = send_list.shape[2]
    total_slots = holder_list * slot_capacity
    listed = send_list[0]
    present = listed >= 0
    safe_rows = jnp.where(present, listed, 0)
    local_ids = tenant % adapters_here
    picked_ids = local_ids[safe_rows]
    adapter_ids = jnp.arange(adapters_here, dtype=jnp.int32)
    selector = (
        (picked_ids[:, :, None] == adapter_ids[None, None, :]) & present[:, :, None]
    ).astype(jnp.bfloat16)
    send_x = tokens[safe_rows]
    send_dy = cotangent[safe_rows]
    drop_rows = jnp.where(present, listed, rows_here).reshape(total_slots)
    fsdp_pos = lax.axis_index("fsdp")
    selected_half = fsdp_pos * column_span // KV
    weight_cols = base_weight
    local_base_output = lax.psum_scatter(
        lax.dot_general(
            weight_cols, tokens, (((0,), (1,)), ((), ())), preferred_element_type=jnp.float32
        ),
        "fsdp",
        scatter_dimension=0,
        tiled=True,
    ).T
    weight_cols = base_weight
    input_frozen_part = lax.dot_general(
        lax.all_gather(cotangent, "fsdp", axis=1, tiled=True),
        weight_cols,
        (((1,), (1,)), ((), ())),
        preferred_element_type=jnp.float32,
    )
    recv_x, recv_sel = (
        lax.all_to_all(send_x, "adapter", split_axis=0, concat_axis=0, tiled=True),
        lax.all_to_all(selector, "adapter", split_axis=0, concat_axis=0, tiled=True),
    )
    input_rows = recv_x.reshape(total_slots, width_here)
    weight_table = recv_sel.reshape(total_slots, adapters_here)
    weights_f = weight_table.astype(jnp.float32)
    low_term = down_partial(input_rows, weights_f, down_weight)
    reduced_rank_sum = lax.psum(low_term, "fsdp")
    adapter_update, broadcast_rows = forward_holder(
        reduced_rank_sum.astype(jnp.bfloat16), weight_table, up_projection_weight, selected_half
    )
    got_delta = lax.all_to_all(
        adapter_update.reshape(holder_list, slot_capacity, column_span),
        "adapter",
        split_axis=0,
        concat_axis=0,
        tiled=True,
    )
    recv_dy = lax.all_to_all(send_dy, "adapter", split_axis=0, concat_axis=0, tiled=True)
    rows_dy = recv_dy.reshape(total_slots, column_span)
    back_sum = lax.psum(
        grad_partial(rows_dy, weights_f, up_projection_weight, selected_half), "fsdp"
    )
    backward_update, down_weight_gradient, up_weight_gradient = backward_owner(
        back_sum.astype(jnp.bfloat16),
        weight_table,
        input_rows,
        rows_dy,
        broadcast_rows,
        down_weight,
    )
    got_back = lax.all_to_all(
        backward_update.reshape(holder_list, slot_capacity, width_here),
        "adapter",
        split_axis=0,
        concat_axis=0,
        tiled=True,
    )
    adapter_columns = (
        jnp.zeros((rows_here, column_span), jnp.float32)
        .at[drop_rows]
        .add(got_delta.reshape(total_slots, column_span).astype(jnp.float32), mode="drop")
    )
    projected = (local_base_output + adapter_columns).astype(jnp.bfloat16)
    adapter_backward = (
        jnp.zeros((rows_here, width_here), jnp.float32)
        .at[drop_rows]
        .add(got_back.reshape(total_slots, width_here).astype(jnp.float32), mode="drop")
    )
    token_gradient = (input_frozen_part + adapter_backward).astype(jnp.bfloat16)
    return (projected, token_gradient, down_weight_gradient, up_weight_gradient)

BF16 = jnp.bfloat16
F32 = jnp.float32
MIB = 1 << 20
HINT_FLOPS, HINT_BYTES = 1 << 10, 1 << 10


def contract(left, right, left_dim, right_dim):
    return lax.dot_general(
        left, right, (((left_dim,), (right_dim,)), ((), ())), preferred_element_type=F32
    )


def swap(value, axis, bits):
    size = lax.axis_size(axis)
    return lax.ppermute(value, axis, [(i, i ^ bits) for i in range(size)])


def call(body, name, outs, args, *, grid=(), in_specs=None, out_specs=None, scratch=(), scalars=0, vmem=12, needs=(), passed=None):
    given = len(args)
    extra = [*needs] + ([passed] if passed is not None else [])
    in_specs = list(in_specs) if in_specs is not None else [pl.BlockSpec()] * (given - scalars)
    out_specs = list(out_specs) if out_specs is not None else [pl.BlockSpec()] * len(outs)
    anywhere = pl.BlockSpec(memory_space=pl.ANY)
    count = len(outs)
    aliases = {}
    if passed is not None:
        outs = [*outs, shape(passed.shape, passed.dtype)]
        out_specs.append(anywhere)
        aliases = {given + len(extra) - 1: count}

    def run(*refs):
        kept = refs[:given] + refs[given + len(extra) : given + len(extra) + count]
        body(*kept, *refs[given + len(extra) + len(outs) :])

    spec = pltpu.PrefetchScalarGridSpec(
        num_scalar_prefetch=scalars,
        grid=grid,
        in_specs=in_specs + [anywhere] * len(extra),
        out_specs=out_specs,
        scratch_shapes=list(scratch),
    )
    return pl.pallas_call(
        run,
        grid_spec=spec,
        out_shape=outs,
        name=name,
        input_output_aliases=aliases,
        cost_estimate=pl.CostEstimate(flops=HINT_FLOPS, bytes_accessed=HINT_BYTES, transcendentals=0),
        compiler_params=pltpu.CompilerParams(vmem_limit_bytes=vmem * MIB),
    )(*args, *extra)


def tie(values, needs):
    count, total = len(values), len(values) + len(needs)
    anywhere = pl.BlockSpec(memory_space=pl.ANY)
    return pl.pallas_call(
        lambda *refs: None,
        in_specs=[anywhere] * total,
        out_specs=[anywhere] * count,
        out_shape=[shape(v.shape, v.dtype) for v in values],
        name="tie",
        input_output_aliases={i: i for i in range(count)},
        cost_estimate=pl.CostEstimate(flops=HINT_FLOPS, bytes_accessed=HINT_BYTES, transcendentals=0),
        compiler_params=pltpu.CompilerParams(vmem_limit_bytes=MIB),
    )(*values, *needs)


def shape(dims, dtype=BF16):
    return jax.ShapeDtypeStruct(dims, dtype)


ORDER = (0, 1, 6, 7, 4, 5, 2, 3)


def after(value, *others):
    return lax.optimization_barrier((value, *others))[0]


def back_body(holders, capacity, rank, local, *refs):
    messages, up_ref = refs[:holders], refs[holders]
    dy_ref, ids_ref, own_ref, mate_ref, part_ref = refs[holders + 1 :]
    me = lax.axis_index("adapter")
    rows = messages[0].shape[0] - 16
    span = up_ref.shape[2]
    owner = lax.broadcasted_iota(jnp.int32, (holders, capacity), 0)
    row_id = lax.broadcasted_iota(jnp.int32, (rows, capacity), 0).astype(F32)
    upper_lanes = (lax.broadcasted_iota(jnp.int32, (capacity, 2 * rank), 1) >= rank).astype(F32)
    up = up_ref[...].reshape(local * rank, span)
    for g in range(holders):
        tail = messages[g][rows : rows + 16, :capacity].astype(F32)
        lists, ids = tail[:holders], tail[holders:]
        listed = jnp.sum(jnp.where(owner == me, lists, 0.0), axis=0, keepdims=True)
        pick = (row_id == listed).astype(F32).astype(BF16)
        own_ref[g] = pick
        if g % 2 == 0:
            other = jnp.sum(jnp.where(owner == (me ^ 1), lists, 0.0), axis=0, keepdims=True)
            mate_ref[g // 2] = (row_id == other).astype(F32).astype(BF16)
        column = ids.T
        adapter = jnp.concatenate([column[:, j : j + 1] for j in range(rows // capacity)], axis=0)
        adapter = jnp.broadcast_to(adapter + 1.0, (rows, capacity)).astype(BF16)
        ids = contract(pick, adapter, 0, 0)
        ids_ref[g] = ids
        dy = contract(pick, messages[g][:rows, :], 0, 0).astype(BF16)
        dy_ref[g] = dy
        wide = contract(dy, up, 1, 1)
        total = jnp.zeros((capacity, 2 * rank), F32)
        for p in range(local // 2):
            wanted = upper_lanes + (2 * p + 1.0)
            total += jnp.where(ids == wanted, wide[:, 2 * rank * p : 2 * rank * (p + 1)], 0.0)
        part_ref[g] = total[:, :rank] + total[:, rank:]


def place_body(upper_ref, odd_ref):
    place = lax.axis_index("fsdp")
    upper_ref[...] = jnp.full(upper_ref.shape, (place >= lax.axis_size("fsdp") // 2).astype(F32))
    odd_ref[...] = jnp.full(odd_ref.shape, (place & 1).astype(F32))


def low_body(local, count, first, *refs):
    blocks = refs[: 2 * count]
    own_ref, ids_ref, down_ref, slots_ref, part_ref = refs[2 * count :]
    half = blocks[0].shape[0]
    capacity = own_ref.shape[2]
    width = down_ref.shape[2]
    for j in range(count):
        picked = contract(own_ref[first + j, :half], blocks[2 * j][...], 0, 0)
        picked += contract(own_ref[first + j, half:], blocks[2 * j + 1][...], 0, 0)
        slots_ref[j * capacity : (j + 1) * capacity, :] = picked.astype(BF16)
    ids = ids_ref[first : first + count].reshape(count * capacity, capacity)
    total = jnp.zeros((count * capacity, width), F32)
    for a in range(0, local, 2):
        weights = jnp.concatenate([down_ref[a], down_ref[a + 1]], axis=1)
        wide = contract(slots_ref[...], weights, 1, 0)
        total += jnp.where(ids == a + 1.0, wide[:, :width], 0.0)
        total += jnp.where(ids == a + 2.0, wide[:, width:], 0.0)
    part_ref[...] = total


def spread(low, ids, local):
    low = low.astype(F32)
    return jnp.concatenate([jnp.where(ids == a + 1.0, low, 0.0) for a in range(local)], axis=1).astype(BF16)


def delta_body(local, low_ref, ids_ref, down_ref, odd_ref, even_ref, wide_ref):
    slots = low_ref.shape[0]
    holders, capacity, _ = ids_ref.shape

    @pl.when(pl.program_id(0) == 0)
    def _():
        for g in range(holders):
            at = (g % 2) * (slots // 2) + (g // 2) * capacity
            wide_ref[pl.ds(at, capacity), :] = spread(
                low_ref[g * capacity : (g + 1) * capacity, :], ids_ref[g], local
            )

    weights = jnp.concatenate([down_ref[a] for a in range(local)], axis=1)
    half = slots // 2
    for part, out_ref in ((1, odd_ref), (0, even_ref)):
        out = (adapter_scale * contract(wide_ref[pl.ds(part * half, half), :], weights, 1, 1)).astype(BF16)
        out_ref[...] = out.reshape(half // capacity, capacity, out.shape[1])


def up_body(local, low_ref, ids_ref, up_ref, odd_ref, even_ref, wide_ref):
    slots, rank = low_ref.shape
    holders, capacity, _ = ids_ref.shape
    low = low_ref[...].astype(F32)
    low = jnp.concatenate([low, low], axis=1)
    ids = ids_ref[...].reshape(slots, capacity)
    upper_lanes = (lax.broadcasted_iota(jnp.int32, (slots, 2 * rank), 1) >= rank).astype(F32)
    wide = jnp.concatenate(
        [jnp.where(ids == upper_lanes + (2 * p + 1.0), low, 0.0) for p in range(local // 2)], axis=1
    ).astype(BF16)
    wide_ref[...] = wide
    span = up_ref.shape[2]
    up = up_ref[...].reshape(local * rank, span)
    out = (adapter_scale * contract(wide, up, 1, 0)).astype(BF16)
    for g in range(holders):
        (odd_ref if g % 2 else even_ref)[g // 2] = out[g * capacity : (g + 1) * capacity]


def expand_body(picks, own_ref, mate_ref, even_ref, got_ref, *out_refs):
    for (p, first, count), out_ref in zip(picks, out_refs):
        pick = jnp.concatenate(
            [own_ref[2 * p][first : first + count], mate_ref[p][first : first + count]], axis=1
        )
        both = jnp.concatenate([even_ref[p], got_ref[p]], axis=0)
        out_ref[...] = contract(pick, both, 1, 0).astype(BF16)


def expand(name, start, pairs, picks, own, mate, even, got, step, needs=()):
    rows, capacity = own.shape[1:]
    width = even.shape[2]
    step = min(width, step)
    block = start // pairs
    return call(
        lambda *refs: expand_body(picks, *refs),
        name,
        [shape((count, width)) for _, _, count in picks],
        [own, mate, even, got],
        grid=(width // step,),
        in_specs=[
            pl.BlockSpec((2 * pairs, rows, capacity), lambda i: (block, 0, 0)),
            pl.BlockSpec((pairs, rows, capacity), lambda i: (block, 0, 0)),
            pl.BlockSpec((pairs, capacity, step), lambda i: (block, 0, i)),
            pl.BlockSpec((pairs, capacity, step), lambda i: (block, 0, i)),
        ],
        out_specs=[pl.BlockSpec((count, step), lambda i: (0, i)) for _, _, count in picks],
        needs=needs,
    )


def down_grad_body(local, pieces, *refs):
    blocks = refs[:pieces]
    low_ref, ids_ref, out_ref, wide_ref = refs[pieces:]
    slots = low_ref.shape[0]

    @pl.when(pl.program_id(0) == 0)
    def _():
        wide_ref[...] = spread(low_ref[...], ids_ref[...].reshape(slots, -1), local)

    rows = jnp.concatenate([block[...] for block in blocks], axis=0)
    out = (adapter_scale * contract(rows, wide_ref[...], 0, 0)).astype(BF16)
    width = low_ref.shape[1]
    for a in range(local):
        out_ref[a] = out[:, a * width : (a + 1) * width]


def shards(tokens, tenant, send_list, base_weight, down_weight, up_weight, cotangent):
    rows, width = tokens.shape
    span = cotangent.shape[1]
    local, _, pair = down_weight.shape
    rank = up_weight.shape[1]
    holders, capacity = send_list.shape[1], send_list.shape[2]
    slots = holders * capacity
    fsdp = lax.axis_size("fsdp")
    upper, odd_place = call(place_body, "place", [shape((8, 128), F32)] * 2, [], vmem=1)

    def where(mask, yes, no):
        mask = jnp.broadcast_to(mask[:1, :1], yes.shape)
        return jnp.where(mask > 0.5, yes, no)
    half = rows // 2
    chunk = 512

    extra = jnp.concatenate([send_list[0], (tenant % local).reshape(-1, capacity)], axis=0).astype(BF16)
    extra = jnp.pad(extra, ((0, 16 - extra.shape[0]), (0, span - capacity)))
    message = jnp.concatenate([cotangent, extra], axis=0)
    near = {0: message}
    for bits in (2, 4, 6):
        near[bits] = swap(message, "adapter", bits)
    top, bottom = tokens[:half], tokens[half:]
    base_partial = jnp.dot(tokens, base_weight, preferred_element_type=F32).astype(BF16)
    near[2], near[4], near[6], top = tie((near[2], near[4], near[6], top), (base_partial,))
    messages = []
    for bits in ORDER[::2]:
        messages += [near[bits], swap(near[bits], "adapter", 1)]
    far_dy = swap(cotangent, "fsdp", 2)
    slots_dy, ids, own, mate, back_part = call(
        lambda *refs: back_body(holders, capacity, rank, local, *refs),
        "back_rows",
        [
            shape((holders, capacity, span)),
            shape((holders, capacity, capacity), F32),
            shape((holders, rows, capacity)),
            shape((holders // 2, rows, capacity)),
            shape((holders, capacity, rank), F32),
        ],
        [*messages, up_weight],
    )
    back_part = back_part.reshape(slots, rank)
    flat_ids = ids.reshape(slots, capacity)

    def low_rows(first, blocks, needs=()):
        count = len(blocks)
        return call(
            lambda *refs: low_body(local, count, first, *refs),
            "low_rows",
            [shape((count * capacity, width)), shape((count * capacity, pair), F32)],
            [*sum(blocks, ()), own, ids, down_weight],
            vmem=16,
            needs=needs,
        )

    def with_mates(*blocks):
        out = []
        for block in blocks:
            out += [block, tuple(swap(piece, "adapter", 1) for piece in block)]
        return out

    got1 = swap(back_part.astype(BF16), "fsdp", 1)
    x_top, y_top = swap(top, "adapter", 2), swap(top, "adapter", 4)
    x_a, low_a = low_rows(0, with_mates((top, bottom)))
    back_half = (back_part + got1.astype(F32)).astype(BF16)
    (back_half,) = tie((back_half,), (x_top, y_top, low_a, far_dy))

    back_other = swap(back_half, "fsdp", 2)
    x_bottom, y_bottom = swap(bottom, "adapter", 2), swap(bottom, "adapter", 4)
    next_dy = swap(cotangent, "fsdp", 1), swap(far_dy, "fsdp", 1)
    back_low = where(
        upper,
        jnp.concatenate([back_other, back_half], axis=1),
        jnp.concatenate([back_half, back_other], axis=1),
    )
    odd, even = call(
        lambda *refs: delta_body(local, *refs),
        "back_delta",
        [shape((holders // 2, capacity, width))] * 2,
        [back_low, ids, down_weight],
        grid=(width // chunk,),
        in_specs=[
            pl.BlockSpec((slots, pair), lambda i: (0, 0)),
            pl.BlockSpec((holders, capacity, capacity), lambda i: (0, 0, 0)),
            pl.BlockSpec((local, chunk, pair), lambda i: (0, i, 0)),
        ],
        out_specs=[pl.BlockSpec((holders // 2, capacity, chunk), lambda i: (0, 0, i))] * 2,
        scratch=[pltpu.VMEM((slots, local * pair), BF16)],
        vmem=16,
        needs=(x_bottom, y_bottom, *next_dy),
    )

    got = swap(odd, "adapter", 1)
    diag = (swap(y_top, "adapter", 2), swap(x_bottom, "adapter", 4))
    x_b, low_b = low_rows(4, with_mates((y_top, y_bottom), (x_top, x_bottom)))
    x_c, low_c = low_rows(2, with_mates(diag))
    low_part = jnp.concatenate([low_a, low_c, low_b], axis=0)
    keep = where(upper, low_part[:, rank:], low_part[:, :rank])
    give = where(upper, low_part[:, :rank], low_part[:, rank:]).astype(BF16)
    diag_low, diag_high = expand(
        "back_diag", 1, 1, ((0, 0, half), (0, half, half)), own, mate, even, got, 1024, needs=(give,)
    )

    low_in = swap(diag_low, "adapter", 2)
    high_in = swap(diag_high, "adapter", 4)
    got_low = swap(give, "fsdp", 2)
    y_low, y_high, x_low, x_high = expand(
        "back_near",
        2,
        2,
        ((0, 0, half), (0, half, half), (1, 0, half), (1, half, half)),
        own,
        mate,
        even,
        got,
        1024,
    )
    (down_grad,) = call(
        lambda *refs: down_grad_body(local, 3, *refs),
        "down_grad",
        [shape((local, width, pair))],
        [x_a, x_c, x_b, back_low, flat_ids],
        grid=(width // 256,),
        in_specs=[pl.BlockSpec((x.shape[0], 256), lambda i: (0, i)) for x in (x_a, x_c, x_b)]
        + [pl.BlockSpec((slots, pair), lambda i: (0, 0)), pl.BlockSpec((slots, capacity), lambda i: (0, 0))],
        out_specs=[pl.BlockSpec((local, 256, pair), lambda i: (0, i, 0))],
        scratch=[pltpu.VMEM((slots, local * pair), BF16)],
        vmem=16,
    )
    quarter = [base_partial[:, i * span : (i + 1) * span] for i in range(4)]
    base_keep = [where(odd_place, quarter[1], quarter[0]), where(odd_place, quarter[3], quarter[2])]
    base_give = [where(odd_place, quarter[0], quarter[1]), where(odd_place, quarter[2], quarter[3])]
    base_got = swap(jnp.concatenate(base_give, axis=1), "fsdp", 1)
    to_y, to_x = y_low + low_in, x_high + high_in
    low_sum = keep + got_low.astype(F32)
    (low_sent,) = tie((low_sum.astype(BF16),), (to_y, to_x, down_grad, base_got))

    got2 = swap(low_sent, "fsdp", 1)
    high_from_y = swap(y_high, "adapter", 4)
    low_from_x = swap(x_low, "adapter", 2)
    ordered = [
        where(odd_place, b, a) for a, b in ((cotangent, next_dy[0]), (next_dy[0], cotangent))
    ], [where(odd_place, b, a) for a, b in ((far_dy, next_dy[1]), (next_dy[1], far_dy))]
    all_dy = jnp.concatenate(
        [where(upper, ordered[1 - i][j], ordered[i][j]) for i in range(2) for j in range(2)], axis=1
    )
    input_base = contract(all_dy, base_weight, 1, 1)
    (home,) = expand("back_home", 0, 1, ((0, 0, rows),), own, mate, even, got, 1024)
    low_half = (low_sum + got2.astype(F32)).astype(BF16)
    up_odd, up_even, wide_low = call(
        lambda *refs: up_body(local, *refs),
        "up_delta",
        [shape((holders // 2, capacity, span))] * 2 + [shape((slots, local * rank))],
        [low_half, ids, up_weight],
        needs=(input_base, home, high_from_y, low_from_x),
    )

    low_from_y = swap(to_y, "adapter", 4)
    high_from_x = swap(to_x, "adapter", 2)
    base_sum = [
        base_keep[i].astype(F32) + base_got[:, i * span : (i + 1) * span].astype(F32) for i in range(2)
    ]
    base_far = swap(where(upper, base_sum[0], base_sum[1]).astype(BF16), "fsdp", 2)
    base_out = where(upper, base_sum[1], base_sum[0]) + base_far.astype(F32)
    up_got = swap(up_odd, "adapter", 1)
    add_home, add_diag, add_y, add_x = expand(
        "up_rows", 0, 4, tuple((p, 0, rows) for p in range(4)), own, mate, up_even, up_got, 512
    )
    add_x = swap(add_x, "adapter", 2)
    add_y = swap(add_y, "adapter", 4)
    add_diag = swap(add_diag, "adapter", 6)
    up_grad = adapter_scale * contract(wide_low, slots_dy.reshape(slots, span), 0, 0)
    up_grad = up_grad.astype(BF16).reshape(local, rank, span)

    projected = (base_out + (add_home + add_x + add_y + add_diag).astype(F32)).astype(BF16)
    low_rows_out = home[:half] + low_from_x + low_from_y
    high_rows_out = home[half:] + high_from_x + high_from_y
    token_gradient = (
        input_base + jnp.concatenate([low_rows_out, high_rows_out], axis=0).astype(F32)
    ).astype(BF16)
    return (projected, token_gradient, down_grad, up_grad)


def solution(mesh):
    in_specs = (
        P("adapter", "fsdp"),
        P("adapter"),
        P("adapter", None, None),
        P("fsdp", None),
        P("adapter", "fsdp", None),
        P("adapter", None, "fsdp"),
        P("adapter", "fsdp"),
    )
    out_specs = (
        P("adapter", "fsdp"),
        P("adapter", "fsdp"),
        P("adapter", "fsdp", None),
        P("adapter", None, "fsdp"),
    )
    program = shards if mesh.shape["adapter"] == 8 and mesh.shape["fsdp"] == 4 else shards_any
    return jax.shard_map(program, mesh=mesh, in_specs=in_specs, out_specs=out_specs, check_vma=False)
```

```python
import jax
import jax.numpy as jnp
from jax import lax
from jax.experimental import pallas as pl
from jax.experimental.pallas import tpu as pltpu
from jax.sharding import PartitionSpec as P

KV = 1024


adapter_scale = 0.5


def down_partial(input_rows, weights_f, down_weight):
    low_all = jnp.einsum("sd,ldk->slk", input_rows, down_weight, preferred_element_type=jnp.float32)
    return jnp.sum(low_all * weights_f[:, :, None], axis=1)


def grad_partial(rows_dy, weights_f, up_projection_weight, selected_half):
    rank_size = up_projection_weight.shape[1]
    back_all = jnp.einsum(
        "sc,lrc->slr", rows_dy, up_projection_weight, preferred_element_type=jnp.float32
    )
    half_sum = jnp.sum(back_all * weights_f[:, :, None], axis=1)
    placed = jnp.zeros((rows_dy.shape[0], 2 * rank_size), jnp.float32)
    zero_idx = jnp.zeros((), jnp.int32)
    return lax.dynamic_update_slice(placed, half_sum, (zero_idx, selected_half * rank_size))


def forward_holder(low_rank, weight_table, up_projection_weight, selected_half):
    rank_size = up_projection_weight.shape[1]
    low_half = lax.dynamic_slice_in_dim(low_rank, selected_half * rank_size, rank_size, 1)
    broadcast_rows = low_half[:, None, :] * weight_table[:, :, None]
    adapter_update = adapter_scale * jnp.einsum(
        "slr,lrc->sc", broadcast_rows, up_projection_weight, preferred_element_type=jnp.float32
    )
    return (adapter_update.astype(jnp.bfloat16), broadcast_rows)


def backward_owner(back_low, weight_table, input_rows, rows_dy, broadcast_rows, down_weight):
    widened_rows = back_low[:, None, :] * weight_table[:, :, None]
    backward_update = adapter_scale * jnp.einsum(
        "wnr,nyr->wy", widened_rows, down_weight, preferred_element_type=jnp.float32
    )
    down_weight_gradient = adapter_scale * jnp.einsum(
        "wq,wmu->mqu", input_rows, widened_rows, preferred_element_type=jnp.float32
    )
    up_weight_gradient = adapter_scale * jnp.einsum(
        "slr,sc->lrc", broadcast_rows, rows_dy, preferred_element_type=jnp.float32
    )
    return (
        backward_update.astype(jnp.bfloat16),
        down_weight_gradient.astype(jnp.bfloat16),
        up_weight_gradient.astype(jnp.bfloat16),
    )


def shards_any(tokens, tenant, send_list, base_weight, down_weight, up_projection_weight, cotangent):
    rows_here = tokens.shape[0]
    width_here = tokens.shape[1]
    column_span = cotangent.shape[1]
    adapters_here = down_weight.shape[0]
    holder_list = send_list.shape[1]
    slot_capacity = send_list.shape[2]
    total_slots = holder_list * slot_capacity
    listed = send_list[0]
    present = listed >= 0
    safe_rows = jnp.where(present, listed, 0)
    local_ids = tenant % adapters_here
    picked_ids = local_ids[safe_rows]
    adapter_ids = jnp.arange(adapters_here, dtype=jnp.int32)
    selector = (
        (picked_ids[:, :, None] == adapter_ids[None, None, :]) & present[:, :, None]
    ).astype(jnp.bfloat16)
    send_x = tokens[safe_rows]
    send_dy = cotangent[safe_rows]
    drop_rows = jnp.where(present, listed, rows_here).reshape(total_slots)
    fsdp_pos = lax.axis_index("fsdp")
    selected_half = fsdp_pos * column_span // KV
    weight_cols = base_weight
    local_base_output = lax.psum_scatter(
        lax.dot_general(
            weight_cols, tokens, (((0,), (1,)), ((), ())), preferred_element_type=jnp.float32
        ),
        "fsdp",
        scatter_dimension=0,
        tiled=True,
    ).T
    weight_cols = base_weight
    input_frozen_part = lax.dot_general(
        lax.all_gather(cotangent, "fsdp", axis=1, tiled=True),
        weight_cols,
        (((1,), (1,)), ((), ())),
        preferred_element_type=jnp.float32,
    )
    recv_x, recv_sel = (
        lax.all_to_all(send_x, "adapter", split_axis=0, concat_axis=0, tiled=True),
        lax.all_to_all(selector, "adapter", split_axis=0, concat_axis=0, tiled=True),
    )
    input_rows = recv_x.reshape(total_slots, width_here)
    weight_table = recv_sel.reshape(total_slots, adapters_here)
    weights_f = weight_table.astype(jnp.float32)
    low_term = down_partial(input_rows, weights_f, down_weight)
    reduced_rank_sum = lax.psum(low_term, "fsdp")
    adapter_update, broadcast_rows = forward_holder(
        reduced_rank_sum.astype(jnp.bfloat16), weight_table, up_projection_weight, selected_half
    )
    got_delta = lax.all_to_all(
        adapter_update.reshape(holder_list, slot_capacity, column_span),
        "adapter",
        split_axis=0,
        concat_axis=0,
        tiled=True,
    )
    recv_dy = lax.all_to_all(send_dy, "adapter", split_axis=0, concat_axis=0, tiled=True)
    rows_dy = recv_dy.reshape(total_slots, column_span)
    back_sum = lax.psum(
        grad_partial(rows_dy, weights_f, up_projection_weight, selected_half), "fsdp"
    )
    backward_update, down_weight_gradient, up_weight_gradient = backward_owner(
        back_sum.astype(jnp.bfloat16),
        weight_table,
        input_rows,
        rows_dy,
        broadcast_rows,
        down_weight,
    )
    got_back = lax.all_to_all(
        backward_update.reshape(holder_list, slot_capacity, width_here),
        "adapter",
        split_axis=0,
        concat_axis=0,
        tiled=True,
    )
    adapter_columns = (
        jnp.zeros((rows_here, column_span), jnp.float32)
        .at[drop_rows]
        .add(got_delta.reshape(total_slots, column_span).astype(jnp.float32), mode="drop")
    )
    projected = (local_base_output + adapter_columns).astype(jnp.bfloat16)
    adapter_backward = (
        jnp.zeros((rows_here, width_here), jnp.float32)
        .at[drop_rows]
        .add(got_back.reshape(total_slots, width_here).astype(jnp.float32), mode="drop")
    )
    token_gradient = (input_frozen_part + adapter_backward).astype(jnp.bfloat16)
    return (projected, token_gradient, down_weight_gradient, up_weight_gradient)

BF16 = jnp.bfloat16
F32 = jnp.float32
MIB = 1 << 20
HINT_FLOPS, HINT_BYTES = 1 << 10, 1 << 10


def contract(left, right, left_dim, right_dim):
    return lax.dot_general(
        left, right, (((left_dim,), (right_dim,)), ((), ())), preferred_element_type=F32
    )


def swap(value, axis, bits):
    size = lax.axis_size(axis)
    return lax.ppermute(value, axis, [(i, i ^ bits) for i in range(size)])


def call(body, name, outs, args, *, grid=(), in_specs=None, out_specs=None, scratch=(), scalars=0, vmem=12, needs=(), passed=None, hint=1):
    given = len(args)
    extra = [*needs] + ([passed] if passed is not None else [])
    in_specs = list(in_specs) if in_specs is not None else [pl.BlockSpec()] * (given - scalars)
    out_specs = list(out_specs) if out_specs is not None else [pl.BlockSpec()] * len(outs)
    anywhere = pl.BlockSpec(memory_space=pl.ANY)
    count = len(outs)
    aliases = {}
    if passed is not None:
        outs = [*outs, shape(passed.shape, passed.dtype)]
        out_specs.append(anywhere)
        aliases = {given + len(extra) - 1: count}

    def run(*refs):
        kept = refs[:given] + refs[given + len(extra) : given + len(extra) + count]
        body(*kept, *refs[given + len(extra) + len(outs) :])

    spec = pltpu.PrefetchScalarGridSpec(
        num_scalar_prefetch=scalars,
        grid=grid,
        in_specs=in_specs + [anywhere] * len(extra),
        out_specs=out_specs,
        scratch_shapes=list(scratch),
    )
    return pl.pallas_call(
        run,
        grid_spec=spec,
        out_shape=outs,
        name=name,
        input_output_aliases=aliases,
        cost_estimate=pl.CostEstimate(
            flops=HINT_FLOPS * hint, bytes_accessed=HINT_BYTES * hint, transcendentals=0
        ),
        compiler_params=pltpu.CompilerParams(vmem_limit_bytes=vmem * MIB),
    )(*args, *extra)


def tie(values, needs):
    count, total = len(values), len(values) + len(needs)
    anywhere = pl.BlockSpec(memory_space=pl.ANY)
    return pl.pallas_call(
        lambda *refs: None,
        in_specs=[anywhere] * total,
        out_specs=[anywhere] * count,
        out_shape=[shape(v.shape, v.dtype) for v in values],
        name="tie",
        input_output_aliases={i: i for i in range(count)},
        cost_estimate=pl.CostEstimate(flops=HINT_FLOPS, bytes_accessed=HINT_BYTES, transcendentals=0),
        compiler_params=pltpu.CompilerParams(vmem_limit_bytes=MIB),
    )(*values, *needs)


def shape(dims, dtype=BF16):
    return jax.ShapeDtypeStruct(dims, dtype)


ORDER = (0, 1, 6, 7, 4, 5, 2, 3)


def after(value, *others):
    return lax.optimization_barrier((value, *others))[0]


def back_body(holders, capacity, rank, local, *refs):
    messages, up_ref = refs[:holders], refs[holders]
    dy_ref, ids_ref, own_ref, mate_ref, part_ref = refs[holders + 1 :]
    me = lax.axis_index("adapter")
    rows = messages[0].shape[0] - 16
    span = up_ref.shape[2]
    owner = lax.broadcasted_iota(jnp.int32, (holders, capacity), 0)
    row_id = lax.broadcasted_iota(jnp.int32, (rows, capacity), 0).astype(F32)
    upper_lanes = (lax.broadcasted_iota(jnp.int32, (capacity, 2 * rank), 1) >= rank).astype(F32)
    up = up_ref[...].reshape(local * rank, span)
    for g in range(holders):
        tail = messages[g][rows : rows + 16, :capacity].astype(F32)
        lists, ids = tail[:holders], tail[holders:]
        listed = jnp.sum(jnp.where(owner == me, lists, 0.0), axis=0, keepdims=True)
        pick = (row_id == listed).astype(F32).astype(BF16)
        own_ref[g] = pick
        if g % 2 == 0:
            other = jnp.sum(jnp.where(owner == (me ^ 1), lists, 0.0), axis=0, keepdims=True)
            mate_ref[g // 2] = (row_id == other).astype(F32).astype(BF16)
        column = ids.T
        adapter = jnp.concatenate([column[:, j : j + 1] for j in range(rows // capacity)], axis=0)
        adapter = jnp.broadcast_to(adapter + 1.0, (rows, capacity)).astype(BF16)
        ids = contract(pick, adapter, 0, 0)
        ids_ref[g] = ids
        dy = contract(pick, messages[g][:rows, :], 0, 0).astype(BF16)
        dy_ref[g] = dy
        wide = contract(dy, up, 1, 1)
        total = jnp.zeros((capacity, 2 * rank), F32)
        for p in range(local // 2):
            wanted = upper_lanes + (2 * p + 1.0)
            total += jnp.where(ids == wanted, wide[:, 2 * rank * p : 2 * rank * (p + 1)], 0.0)
        part_ref[g] = total[:, :rank] + total[:, rank:]


def message_body(local, dy_ref, lists_ref, tenant_ref, out_ref):
    rows, span = dy_ref.shape
    _, holders, capacity = lists_ref.shape
    count = tenant_ref.shape[0]
    out_ref[:rows, :] = dy_ref[...]
    ids = lax.rem(tenant_ref[...], local).astype(F32)
    tail = jnp.concatenate([lists_ref[0].astype(F32), ids, jnp.zeros((16 - holders - count, capacity), F32)], axis=0)
    tail = jnp.concatenate([tail, jnp.zeros((16, span - capacity), F32)], axis=1)
    out_ref[rows:, :] = tail.astype(BF16)


def place_body(upper_ref, odd_ref):
    place = lax.axis_index("fsdp")
    upper_ref[...] = jnp.full(upper_ref.shape, (place >= lax.axis_size("fsdp") // 2).astype(F32))
    odd_ref[...] = jnp.full(odd_ref.shape, (place & 1).astype(F32))


def low_body(local, count, first, *refs):
    own_ref, ids_ref, down_ref, slots_ref, part_ref = refs[-5:]
    pieces = (len(refs) - 5) // count
    rows = own_ref.shape[1] // pieces
    capacity = own_ref.shape[2]
    width = down_ref.shape[2]
    for j in range(count):
        picked = contract(own_ref[first + j, :rows], refs[pieces * j][...], 0, 0)
        for i in range(1, pieces):
            picked += contract(own_ref[first + j, i * rows : (i + 1) * rows], refs[pieces * j + i][...], 0, 0)
        slots_ref[j * capacity : (j + 1) * capacity, :] = picked.astype(BF16)
    ids = ids_ref[first : first + count].reshape(count * capacity, capacity)
    total = jnp.zeros((count * capacity, width), F32)
    for a in range(0, local, 2):
        weights = jnp.concatenate([down_ref[a], down_ref[a + 1]], axis=1)
        wide = contract(slots_ref[...], weights, 1, 0)
        total += jnp.where(ids == a + 1.0, wide[:, :width], 0.0)
        total += jnp.where(ids == a + 2.0, wide[:, width:], 0.0)
    part_ref[...] = total


def spread(low, ids, local):
    low = low.astype(F32)
    return jnp.concatenate([jnp.where(ids == a + 1.0, low, 0.0) for a in range(local)], axis=1).astype(BF16)


def delta_body(local, low_ref, ids_ref, down_ref, odd_ref, even_ref, wide_ref):
    slots = low_ref.shape[0]
    holders, capacity, _ = ids_ref.shape

    @pl.when(pl.program_id(0) == 0)
    def _():
        for g in range(holders):
            at = (g % 2) * (slots // 2) + (g // 2) * capacity
            wide_ref[pl.ds(at, capacity), :] = spread(
                low_ref[g * capacity : (g + 1) * capacity, :], ids_ref[g], local
            )

    weights = jnp.concatenate([down_ref[a] for a in range(local)], axis=1)
    half = slots // 2
    for part, out_ref in ((1, odd_ref), (0, even_ref)):
        out = (adapter_scale * contract(wide_ref[pl.ds(part * half, half), :], weights, 1, 1)).astype(BF16)
        out_ref[...] = out.reshape(half // capacity, capacity, out.shape[1])


def up_body(local, low_ref, ids_ref, up_ref, odd_ref, even_ref, wide_ref):
    slots, rank = low_ref.shape
    holders, capacity, _ = ids_ref.shape
    low = low_ref[...].astype(F32)
    low = jnp.concatenate([low, low], axis=1)
    ids = ids_ref[...].reshape(slots, capacity)
    upper_lanes = (lax.broadcasted_iota(jnp.int32, (slots, 2 * rank), 1) >= rank).astype(F32)
    wide = jnp.concatenate(
        [jnp.where(ids == upper_lanes + (2 * p + 1.0), low, 0.0) for p in range(local // 2)], axis=1
    ).astype(BF16)
    wide_ref[...] = wide
    span = up_ref.shape[2]
    up = up_ref[...].reshape(local * rank, span)
    out = (adapter_scale * contract(wide, up, 1, 0)).astype(BF16)
    for g in range(holders):
        (odd_ref if g % 2 else even_ref)[g // 2] = out[g * capacity : (g + 1) * capacity]


def expand_body(picks, own_ref, mate_ref, even_ref, got_ref, *out_refs):
    for (p, first, count), out_ref in zip(picks, out_refs):
        pick = jnp.concatenate(
            [own_ref[2 * p][first : first + count], mate_ref[p][first : first + count]], axis=1
        )
        both = jnp.concatenate([even_ref[p], got_ref[p]], axis=0)
        out_ref[...] = contract(pick, both, 1, 0).astype(BF16)


def expand(name, start, pairs, picks, own, mate, even, got, step, needs=()):
    rows, capacity = own.shape[1:]
    width = even.shape[2]
    step = min(width, step)
    block = start // pairs
    return call(
        lambda *refs: expand_body(picks, *refs),
        name,
        [shape((count, width)) for _, _, count in picks],
        [own, mate, even, got],
        grid=(width // step,),
        in_specs=[
            pl.BlockSpec((2 * pairs, rows, capacity), lambda i: (block, 0, 0)),
            pl.BlockSpec((pairs, rows, capacity), lambda i: (block, 0, 0)),
            pl.BlockSpec((pairs, capacity, step), lambda i: (block, 0, i)),
            pl.BlockSpec((pairs, capacity, step), lambda i: (block, 0, i)),
        ],
        out_specs=[pl.BlockSpec((count, step), lambda i: (0, i)) for _, _, count in picks],
        needs=needs,
    )


def down_grad_body(local, pieces, *refs):
    blocks = refs[:pieces]
    low_ref, ids_ref, out_ref, made_ref, wide_ref = refs[pieces:]
    made_ref[...] = jnp.zeros_like(made_ref)
    slots = low_ref.shape[0]

    @pl.when(pl.program_id(0) == 0)
    def _():
        wide_ref[...] = spread(low_ref[...], ids_ref[...].reshape(slots, -1), local)

    rows = jnp.concatenate([block[...] for block in blocks], axis=0)
    out = (adapter_scale * contract(rows, wide_ref[...], 0, 0)).astype(BF16)
    width = low_ref.shape[1]
    for a in range(local):
        out_ref[a] = out[:, a * width : (a + 1) * width]


def shards(tokens, tenant, send_list, base_weight, down_weight, up_weight, cotangent):
    rows, width = tokens.shape
    span = cotangent.shape[1]
    local, _, pair = down_weight.shape
    rank = up_weight.shape[1]
    holders, capacity = send_list.shape[1], send_list.shape[2]
    slots = holders * capacity
    fsdp = lax.axis_size("fsdp")
    upper, odd_place = call(place_body, "place", [shape((8, 128), F32)] * 2, [], vmem=1)

    def where(mask, yes, no):
        mask = jnp.broadcast_to(mask[:1, :1], yes.shape)
        return jnp.where(mask > 0.5, yes, no)
    half = rows // 2
    chunk = 512

    (message,) = call(
        lambda *refs: message_body(local, *refs),
        "message",
        [shape((rows + 16, span))],
        [cotangent, send_list, tenant.reshape(-1, capacity)],
    )
    near = {0: message}
    for bits in (2, 4, 6):
        near[bits] = swap(message, "adapter", bits)
    top, bottom = tokens[:half], tokens[half:]
    base_partial = jnp.dot(tokens, base_weight, preferred_element_type=F32).astype(BF16)
    far_dy = swap(cotangent, "fsdp", 2)
    near[2], near[4], near[6], top = tie((near[2], near[4], near[6], top), (base_partial, far_dy))
    messages = []
    for bits in ORDER[::2]:
        messages += [near[bits], swap(near[bits], "adapter", 1)]
    slots_dy, ids, own, mate, back_part = call(
        lambda *refs: back_body(holders, capacity, rank, local, *refs),
        "back_rows",
        [
            shape((holders, capacity, span)),
            shape((holders, capacity, capacity), F32),
            shape((holders, rows, capacity)),
            shape((holders // 2, rows, capacity)),
            shape((holders, capacity, rank), F32),
        ],
        [*messages, up_weight],
    )
    back_part = back_part.reshape(slots, rank)
    flat_ids = ids.reshape(slots, capacity)

    def low_rows(first, blocks, needs=()):
        count = len(blocks)
        return call(
            lambda *refs: low_body(local, count, first, *refs),
            "low_rows",
            [shape((count * capacity, width)), shape((count * capacity, pair), F32)],
            [*sum(blocks, ()), own, ids, down_weight],
            vmem=16,
            needs=needs,
        )

    def with_mates(*blocks):
        out = []
        for block in blocks:
            out += [block, tuple(swap(piece, "adapter", 1) for piece in block)]
        return out

    got1 = swap(back_part.astype(BF16), "fsdp", 1)
    x_top, y_top = swap(top, "adapter", 2), swap(top, "adapter", 4)
    x_a, low_a = low_rows(0, with_mates((tokens,)))
    back_half = (back_part + got1.astype(F32)).astype(BF16)
    (back_half,) = tie((back_half,), (x_top, y_top, low_a))

    back_other = swap(back_half, "fsdp", 2)
    x_bottom, y_bottom = swap(bottom, "adapter", 2), swap(bottom, "adapter", 4)
    back_low = where(
        upper,
        jnp.concatenate([back_other, back_half], axis=1),
        jnp.concatenate([back_half, back_other], axis=1),
    )
    odd, even = call(
        lambda *refs: delta_body(local, *refs),
        "back_delta",
        [shape((holders // 2, capacity, width))] * 2,
        [back_low, ids, down_weight],
        grid=(width // chunk,),
        in_specs=[
            pl.BlockSpec((slots, pair), lambda i: (0, 0)),
            pl.BlockSpec((holders, capacity, capacity), lambda i: (0, 0, 0)),
            pl.BlockSpec((local, chunk, pair), lambda i: (0, i, 0)),
        ],
        out_specs=[pl.BlockSpec((holders // 2, capacity, chunk), lambda i: (0, 0, i))] * 2,
        scratch=[pltpu.VMEM((slots, local * pair), BF16)],
        vmem=16,
        needs=(x_bottom, y_bottom),
        hint=1 << 14,
    )

    got = swap(odd, "adapter", 1)
    diag = (swap(y_top, "adapter", 2), swap(x_bottom, "adapter", 4))
    x_b, low_b = low_rows(4, with_mates((y_top, y_bottom), (x_top, x_bottom)))
    diag_low, diag_high = expand(
        "back_diag", 1, 1, ((0, 0, half), (0, half, half)), own, mate, even, got, 1024
    )
    y_low, y_high, x_low, x_high = expand(
        "back_near",
        2,
        2,
        ((0, 0, half), (0, half, half), (1, 0, half), (1, half, half)),
        own,
        mate,
        even,
        got,
        1024,
    )
    *diag, base_partial = tie((*diag, base_partial), (low_b, diag_low, y_low))

    low_in = swap(diag_low, "adapter", 2)
    high_in = swap(diag_high, "adapter", 4)
    quarter = [base_partial[:, i * span : (i + 1) * span] for i in range(4)]
    base_keep = [where(odd_place, quarter[1], quarter[0]), where(odd_place, quarter[3], quarter[2])]
    base_give = [where(odd_place, quarter[0], quarter[1]), where(odd_place, quarter[2], quarter[3])]
    base_got = swap(jnp.concatenate(base_give, axis=1), "fsdp", 1)
    x_c, low_c = low_rows(2, with_mates(tuple(diag)))
    low_part = jnp.concatenate([low_a, low_c, low_b], axis=0)
    keep = where(upper, low_part[:, rank:], low_part[:, :rank])
    give = where(upper, low_part[:, :rank], low_part[:, rank:]).astype(BF16)
    to_y, to_x = y_low + low_in, x_high + high_in
    give, y_high, x_low = tie((give, y_high, x_low), (to_y, to_x))

    got_low = swap(give, "fsdp", 2)
    next_dy = swap(jnp.stack([cotangent, far_dy]), "fsdp", 1)
    high_from_y = swap(y_high, "adapter", 4)
    low_from_x = swap(x_low, "adapter", 2)
    down_grad, made = call(
        lambda *refs: down_grad_body(local, 3, *refs),
        "down_grad",
        [shape((local, width, pair)), shape((8, 128), F32)],
        [x_a, x_c, x_b, back_low, flat_ids],
        grid=(width // 256,),
        in_specs=[pl.BlockSpec((x.shape[0], 256), lambda i: (0, i)) for x in (x_a, x_c, x_b)]
        + [pl.BlockSpec((slots, pair), lambda i: (0, 0)), pl.BlockSpec((slots, capacity), lambda i: (0, 0))],
        out_specs=[pl.BlockSpec((local, 256, pair), lambda i: (0, i, 0)), pl.BlockSpec((8, 128), lambda i: (0, 0))],
        scratch=[pltpu.VMEM((slots, local * pair), BF16)],
        vmem=16,
    )
    low_sum = keep + got_low.astype(F32)
    low_sent, base_got, to_y, to_x = tie(
        (low_sum.astype(BF16), base_got, to_y, to_x), (made, next_dy, high_from_y, low_from_x)
    )

    got2 = swap(low_sent, "fsdp", 1)
    low_from_y = swap(to_y, "adapter", 4)
    high_from_x = swap(to_x, "adapter", 2)
    ordered = [
        where(odd_place, b, a) for a, b in ((cotangent, next_dy[0]), (next_dy[0], cotangent))
    ], [where(odd_place, b, a) for a, b in ((far_dy, next_dy[1]), (next_dy[1], far_dy))]
    all_dy = jnp.concatenate(
        [where(upper, ordered[1 - i][j], ordered[i][j]) for i in range(2) for j in range(2)], axis=1
    )
    input_base = contract(all_dy, base_weight, 1, 1)
    (home,) = expand("back_home", 0, 1, ((0, 0, rows),), own, mate, even, got, 1024)
    base_sum = [
        base_keep[i].astype(F32) + base_got[:, i * span : (i + 1) * span].astype(F32) for i in range(2)
    ]
    base_far = swap(where(upper, base_sum[0], base_sum[1]).astype(BF16), "fsdp", 2)
    base_out = where(upper, base_sum[1], base_sum[0]) + base_far.astype(F32)
    low_half = (low_sum + got2.astype(F32)).astype(BF16)
    up_odd, up_even, wide_low, input_base = call(
        lambda *refs: up_body(local, *refs),
        "up_delta",
        [shape((holders // 2, capacity, span))] * 2 + [shape((slots, local * rank))],
        [low_half, ids, up_weight],
        needs=(home, low_from_y, high_from_x, base_far),
        passed=input_base,
    )

    up_got = swap(up_odd, "adapter", 1)
    add_home, add_diag, add_y, add_x = expand(
        "up_rows", 0, 4, tuple((p, 0, rows) for p in range(4)), own, mate, up_even, up_got, 512
    )
    add_x = swap(add_x, "adapter", 2)
    add_y = swap(add_y, "adapter", 4)
    add_diag = swap(add_diag, "adapter", 6)
    up_grad = adapter_scale * contract(wide_low, slots_dy.reshape(slots, span), 0, 0)
    up_grad = up_grad.astype(BF16).reshape(local, rank, span)

    projected = (base_out + (add_home + add_x + add_y + add_diag).astype(F32)).astype(BF16)
    low_rows_out = home[:half] + low_from_x + low_from_y
    high_rows_out = home[half:] + high_from_x + high_from_y
    token_gradient = (
        input_base + jnp.concatenate([low_rows_out, high_rows_out], axis=0).astype(F32)
    ).astype(BF16)
    return (projected, token_gradient, down_grad, up_grad)


def solution(mesh):
    in_specs = (
        P("adapter", "fsdp"),
        P("adapter"),
        P("adapter", None, None),
        P("fsdp", None),
        P("adapter", "fsdp", None),
        P("adapter", None, "fsdp"),
        P("adapter", "fsdp"),
    )
    out_specs = (
        P("adapter", "fsdp"),
        P("adapter", "fsdp"),
        P("adapter", "fsdp", None),
        P("adapter", None, "fsdp"),
    )
    program = shards if mesh.shape["adapter"] == 8 and mesh.shape["fsdp"] == 4 else shards_any
    return jax.shard_map(program, mesh=mesh, in_specs=in_specs, out_specs=out_specs, check_vma=False)
```

```python
import jax
import jax.numpy as jnp
from jax import lax
from jax.experimental import pallas as pl
from jax.experimental.pallas import tpu as pltpu
from jax.sharding import PartitionSpec as P

KV = 1024


adapter_scale = 0.5


def down_partial(input_rows, weights_f, down_weight):
    low_all = jnp.einsum("sd,ldk->slk", input_rows, down_weight, preferred_element_type=jnp.float32)
    return jnp.sum(low_all * weights_f[:, :, None], axis=1)


def grad_partial(rows_dy, weights_f, up_projection_weight, selected_half):
    rank_size = up_projection_weight.shape[1]
    back_all = jnp.einsum(
        "sc,lrc->slr", rows_dy, up_projection_weight, preferred_element_type=jnp.float32
    )
    half_sum = jnp.sum(back_all * weights_f[:, :, None], axis=1)
    placed = jnp.zeros((rows_dy.shape[0], 2 * rank_size), jnp.float32)
    zero_idx = jnp.zeros((), jnp.int32)
    return lax.dynamic_update_slice(placed, half_sum, (zero_idx, selected_half * rank_size))


def forward_holder(low_rank, weight_table, up_projection_weight, selected_half):
    rank_size = up_projection_weight.shape[1]
    low_half = lax.dynamic_slice_in_dim(low_rank, selected_half * rank_size, rank_size, 1)
    broadcast_rows = low_half[:, None, :] * weight_table[:, :, None]
    adapter_update = adapter_scale * jnp.einsum(
        "slr,lrc->sc", broadcast_rows, up_projection_weight, preferred_element_type=jnp.float32
    )
    return (adapter_update.astype(jnp.bfloat16), broadcast_rows)


def backward_owner(back_low, weight_table, input_rows, rows_dy, broadcast_rows, down_weight):
    widened_rows = back_low[:, None, :] * weight_table[:, :, None]
    backward_update = adapter_scale * jnp.einsum(
        "wnr,nyr->wy", widened_rows, down_weight, preferred_element_type=jnp.float32
    )
    down_weight_gradient = adapter_scale * jnp.einsum(
        "wq,wmu->mqu", input_rows, widened_rows, preferred_element_type=jnp.float32
    )
    up_weight_gradient = adapter_scale * jnp.einsum(
        "slr,sc->lrc", broadcast_rows, rows_dy, preferred_element_type=jnp.float32
    )
    return (
        backward_update.astype(jnp.bfloat16),
        down_weight_gradient.astype(jnp.bfloat16),
        up_weight_gradient.astype(jnp.bfloat16),
    )


def shards_any(tokens, tenant, send_list, base_weight, down_weight, up_projection_weight, cotangent):
    rows_here = tokens.shape[0]
    width_here = tokens.shape[1]
    column_span = cotangent.shape[1]
    adapters_here = down_weight.shape[0]
    holder_list = send_list.shape[1]
    slot_capacity = send_list.shape[2]
    total_slots = holder_list * slot_capacity
    listed = send_list[0]
    present = listed >= 0
    safe_rows = jnp.where(present, listed, 0)
    local_ids = tenant % adapters_here
    picked_ids = local_ids[safe_rows]
    adapter_ids = jnp.arange(adapters_here, dtype=jnp.int32)
    selector = (
        (picked_ids[:, :, None] == adapter_ids[None, None, :]) & present[:, :, None]
    ).astype(jnp.bfloat16)
    send_x = tokens[safe_rows]
    send_dy = cotangent[safe_rows]
    drop_rows = jnp.where(present, listed, rows_here).reshape(total_slots)
    fsdp_pos = lax.axis_index("fsdp")
    selected_half = fsdp_pos * column_span // KV
    weight_cols = base_weight
    local_base_output = lax.psum_scatter(
        lax.dot_general(
            weight_cols, tokens, (((0,), (1,)), ((), ())), preferred_element_type=jnp.float32
        ),
        "fsdp",
        scatter_dimension=0,
        tiled=True,
    ).T
    weight_cols = base_weight
    input_frozen_part = lax.dot_general(
        lax.all_gather(cotangent, "fsdp", axis=1, tiled=True),
        weight_cols,
        (((1,), (1,)), ((), ())),
        preferred_element_type=jnp.float32,
    )
    recv_x, recv_sel = (
        lax.all_to_all(send_x, "adapter", split_axis=0, concat_axis=0, tiled=True),
        lax.all_to_all(selector, "adapter", split_axis=0, concat_axis=0, tiled=True),
    )
    input_rows = recv_x.reshape(total_slots, width_here)
    weight_table = recv_sel.reshape(total_slots, adapters_here)
    weights_f = weight_table.astype(jnp.float32)
    low_term = down_partial(input_rows, weights_f, down_weight)
    reduced_rank_sum = lax.psum(low_term, "fsdp")
    adapter_update, broadcast_rows = forward_holder(
        reduced_rank_sum.astype(jnp.bfloat16), weight_table, up_projection_weight, selected_half
    )
    got_delta = lax.all_to_all(
        adapter_update.reshape(holder_list, slot_capacity, column_span),
        "adapter",
        split_axis=0,
        concat_axis=0,
        tiled=True,
    )
    recv_dy = lax.all_to_all(send_dy, "adapter", split_axis=0, concat_axis=0, tiled=True)
    rows_dy = recv_dy.reshape(total_slots, column_span)
    back_sum = lax.psum(
        grad_partial(rows_dy, weights_f, up_projection_weight, selected_half), "fsdp"
    )
    backward_update, down_weight_gradient, up_weight_gradient = backward_owner(
        back_sum.astype(jnp.bfloat16),
        weight_table,
        input_rows,
        rows_dy,
        broadcast_rows,
        down_weight,
    )
    got_back = lax.all_to_all(
        backward_update.reshape(holder_list, slot_capacity, width_here),
        "adapter",
        split_axis=0,
        concat_axis=0,
        tiled=True,
    )
    adapter_columns = (
        jnp.zeros((rows_here, column_span), jnp.float32)
        .at[drop_rows]
        .add(got_delta.reshape(total_slots, column_span).astype(jnp.float32), mode="drop")
    )
    projected = (local_base_output + adapter_columns).astype(jnp.bfloat16)
    adapter_backward = (
        jnp.zeros((rows_here, width_here), jnp.float32)
        .at[drop_rows]
        .add(got_back.reshape(total_slots, width_here).astype(jnp.float32), mode="drop")
    )
    token_gradient = (input_frozen_part + adapter_backward).astype(jnp.bfloat16)
    return (projected, token_gradient, down_weight_gradient, up_weight_gradient)

BF16 = jnp.bfloat16
F32 = jnp.float32
MIB = 1 << 20
HINT_FLOPS, HINT_BYTES = 1 << 10, 1 << 10


def contract(left, right, left_dim, right_dim):
    return lax.dot_general(
        left, right, (((left_dim,), (right_dim,)), ((), ())), preferred_element_type=F32
    )


def swap(value, axis, bits):
    size = lax.axis_size(axis)
    return lax.ppermute(value, axis, [(i, i ^ bits) for i in range(size)])


def call(body, name, outs, args, *, grid=(), in_specs=None, out_specs=None, scratch=(), scalars=0, vmem=12, needs=(), passed=(), hint=1):
    given = len(args)
    extra = [*needs, *passed]
    in_specs = list(in_specs) if in_specs is not None else [pl.BlockSpec()] * (given - scalars)
    out_specs = list(out_specs) if out_specs is not None else [pl.BlockSpec()] * len(outs)
    anywhere = pl.BlockSpec(memory_space=pl.ANY)
    count = len(outs)
    outs = [*outs, *(shape(p.shape, p.dtype) for p in passed)]
    out_specs += [anywhere] * len(passed)
    aliases = {given + len(needs) + i: count + i for i in range(len(passed))}

    def run(*refs):
        kept = refs[:given] + refs[given + len(extra) : given + len(extra) + count]
        body(*kept, *refs[given + len(extra) + len(outs) :])

    spec = pltpu.PrefetchScalarGridSpec(
        num_scalar_prefetch=scalars,
        grid=grid,
        in_specs=in_specs + [anywhere] * len(extra),
        out_specs=out_specs,
        scratch_shapes=list(scratch),
    )
    return pl.pallas_call(
        run,
        grid_spec=spec,
        out_shape=outs,
        name=name,
        input_output_aliases=aliases,
        cost_estimate=pl.CostEstimate(
            flops=HINT_FLOPS * hint, bytes_accessed=HINT_BYTES * hint, transcendentals=0
        ),
        compiler_params=pltpu.CompilerParams(vmem_limit_bytes=vmem * MIB),
    )(*args, *extra)


def tie(values, needs):
    count, total = len(values), len(values) + len(needs)
    anywhere = pl.BlockSpec(memory_space=pl.ANY)
    return pl.pallas_call(
        lambda *refs: None,
        in_specs=[anywhere] * total,
        out_specs=[anywhere] * count,
        out_shape=[shape(v.shape, v.dtype) for v in values],
        name="tie",
        input_output_aliases={i: i for i in range(count)},
        cost_estimate=pl.CostEstimate(flops=HINT_FLOPS, bytes_accessed=HINT_BYTES, transcendentals=0),
        compiler_params=pltpu.CompilerParams(vmem_limit_bytes=MIB),
    )(*values, *needs)


def shape(dims, dtype=BF16):
    return jax.ShapeDtypeStruct(dims, dtype)


ORDER = (0, 1, 6, 7, 4, 5, 2, 3)


def after(value, *others):
    return lax.optimization_barrier((value, *others))[0]


def back_body(holders, capacity, rank, local, *refs):
    messages, up_ref = refs[:holders], refs[holders]
    dy_ref, ids_ref, own_ref, mate_ref, part_ref = refs[holders + 1 :]
    me = lax.axis_index("adapter")
    rows = messages[0].shape[0] - 16
    span = up_ref.shape[2]
    owner = lax.broadcasted_iota(jnp.int32, (holders, capacity), 0)
    row_id = lax.broadcasted_iota(jnp.int32, (rows, capacity), 0).astype(F32)
    upper_lanes = (lax.broadcasted_iota(jnp.int32, (capacity, 2 * rank), 1) >= rank).astype(F32)
    up = up_ref[...].reshape(local * rank, span)
    parts = []
    for g in range(holders):
        tail = messages[g][rows : rows + 16, :capacity].astype(F32)
        lists, ids = tail[:holders], tail[holders:]
        listed = jnp.sum(jnp.where(owner == me, lists, 0.0), axis=0, keepdims=True)
        pick = (row_id == listed).astype(F32).astype(BF16)
        own_ref[g] = pick
        if g % 2 == 0:
            other = jnp.sum(jnp.where(owner == (me ^ 1), lists, 0.0), axis=0, keepdims=True)
            mate_ref[g // 2] = (row_id == other).astype(F32).astype(BF16)
        column = ids.T
        adapter = jnp.concatenate([column[:, j : j + 1] for j in range(rows // capacity)], axis=0)
        adapter = jnp.broadcast_to(adapter + 1.0, (rows, capacity)).astype(BF16)
        ids = contract(pick, adapter, 0, 0)
        ids_ref[g] = ids
        dy = contract(pick, messages[g][:rows, :], 0, 0).astype(BF16)
        dy_ref[g] = dy
        wide = contract(dy, up, 1, 1)
        total = jnp.zeros((capacity, 2 * rank), F32)
        for p in range(local // 2):
            wanted = upper_lanes + (2 * p + 1.0)
            total += jnp.where(ids == wanted, wide[:, 2 * rank * p : 2 * rank * (p + 1)], 0.0)
        parts.append(total[:, :rank] + total[:, rank:])
    for g in range(holders // 2):
        part_ref[g] = jnp.concatenate([parts[g], parts[g + holders // 2]], axis=1)


def message_body(local, dy_ref, lists_ref, tenant_ref, out_ref):
    rows, span = dy_ref.shape
    _, holders, capacity = lists_ref.shape
    count = tenant_ref.shape[0]
    out_ref[:rows, :] = dy_ref[...]
    ids = lax.rem(tenant_ref[...], local).astype(F32)
    tail = jnp.concatenate([lists_ref[0].astype(F32), ids, jnp.zeros((16 - holders - count, capacity), F32)], axis=0)
    tail = jnp.concatenate([tail, jnp.zeros((16, span - capacity), F32)], axis=1)
    out_ref[rows:, :] = tail.astype(BF16)


def place_body(upper_ref, odd_ref):
    place = lax.axis_index("fsdp")
    upper_ref[...] = jnp.full(upper_ref.shape, (place >= lax.axis_size("fsdp") // 2).astype(F32))
    odd_ref[...] = jnp.full(odd_ref.shape, (place & 1).astype(F32))


def low_body(local, count, first, starts, *refs):
    own_ref, ids_ref, down_ref, slots_ref, part_ref = refs[-5:]
    pieces = (len(refs) - 5) // count
    rows = own_ref.shape[1] // pieces
    capacity = own_ref.shape[2]
    width = down_ref.shape[2]
    for j in range(count):
        picked = 0.0
        for i in range(pieces):
            at = starts[pieces * j + i]
            piece = refs[pieces * j + i][at : at + rows, :]
            picked += contract(own_ref[first + j, i * rows : (i + 1) * rows], piece, 0, 0)
        slots_ref[j * capacity : (j + 1) * capacity, :] = picked.astype(BF16)
    ids = ids_ref[first : first + count].reshape(count * capacity, capacity)
    total = jnp.zeros((count * capacity, width), F32)
    for a in range(0, local, 2):
        weights = jnp.concatenate([down_ref[a], down_ref[a + 1]], axis=1)
        wide = contract(slots_ref[...], weights, 1, 0)
        total += jnp.where(ids == a + 1.0, wide[:, :width], 0.0)
        total += jnp.where(ids == a + 2.0, wide[:, width:], 0.0)
    part_ref[...] = total


def spread(low, ids, local):
    low = low.astype(F32)
    return jnp.concatenate([jnp.where(ids == a + 1.0, low, 0.0) for a in range(local)], axis=1).astype(BF16)


def delta_body(local, part, low_ref, ids_ref, down_ref, out_ref, wide_ref):
    holders, capacity, _ = ids_ref.shape

    @pl.when(pl.program_id(0) == 0)
    def _():
        for i, g in enumerate(range(part, holders, 2)):
            wide_ref[i * capacity : (i + 1) * capacity, :] = spread(
                low_ref[g * capacity : (g + 1) * capacity, :], ids_ref[g], local
            )

    weights = jnp.concatenate([down_ref[a] for a in range(local)], axis=1)
    out = (adapter_scale * contract(wide_ref[...], weights, 1, 1)).astype(BF16)
    out_ref[...] = out.reshape(out_ref.shape)


def up_body(local, low_ref, ids_ref, up_ref, odd_ref, even_ref, wide_ref):
    slots, rank = 2 * low_ref.shape[0], low_ref.shape[1] // 2
    holders, capacity, _ = ids_ref.shape
    packed = low_ref[...].astype(F32)
    low = jnp.concatenate(
        [jnp.concatenate([packed[:, i : i + rank]] * 2, axis=1) for i in (0, rank)], axis=0
    )
    ids = ids_ref[...].reshape(slots, capacity)
    upper_lanes = (lax.broadcasted_iota(jnp.int32, (slots, 2 * rank), 1) >= rank).astype(F32)
    wide = jnp.concatenate(
        [jnp.where(ids == upper_lanes + (2 * p + 1.0), low, 0.0) for p in range(local // 2)], axis=1
    ).astype(BF16)
    wide_ref[...] = wide
    span = up_ref.shape[2]
    up = up_ref[...].reshape(local * rank, span)
    out = (adapter_scale * contract(wide, up, 1, 0)).astype(BF16)
    for g in range(holders):
        (odd_ref if g % 2 else even_ref)[g // 2] = out[g * capacity : (g + 1) * capacity]


def expand_body(picks, own_ref, mate_ref, even_ref, got_ref, *out_refs):
    for (p, first, count), out_ref in zip(picks, out_refs):
        pick = jnp.concatenate(
            [own_ref[2 * p][first : first + count], mate_ref[p][first : first + count]], axis=1
        )
        both = jnp.concatenate([even_ref[p], got_ref[p]], axis=0)
        out_ref[...] = contract(pick, both, 1, 0).astype(BF16)


def expand(name, start, pairs, picks, own, mate, even, got, step, needs=()):
    rows, capacity = own.shape[1:]
    width = even.shape[2]
    step = min(width, step)
    block = start // pairs
    return call(
        lambda *refs: expand_body(picks, *refs),
        name,
        [shape((count, width)) for _, _, count in picks],
        [own, mate, even, got],
        grid=(width // step,),
        in_specs=[
            pl.BlockSpec((2 * pairs, rows, capacity), lambda i: (block, 0, 0)),
            pl.BlockSpec((pairs, rows, capacity), lambda i: (block, 0, 0)),
            pl.BlockSpec((pairs, capacity, step), lambda i: (block, 0, i)),
            pl.BlockSpec((pairs, capacity, step), lambda i: (block, 0, i)),
        ],
        out_specs=[pl.BlockSpec((count, step), lambda i: (0, i)) for _, _, count in picks],
        needs=needs,
    )


def down_grad_body(local, pieces, *refs):
    blocks = refs[:pieces]
    low_ref, ids_ref, out_ref, made_ref, wide_ref = refs[pieces:]
    made_ref[...] = jnp.zeros_like(made_ref)
    slots = low_ref.shape[0]

    @pl.when(pl.program_id(0) == 0)
    def _():
        wide_ref[...] = spread(low_ref[...], ids_ref[...].reshape(slots, -1), local)

    rows = jnp.concatenate([block[...] for block in blocks], axis=0)
    out = (adapter_scale * contract(rows, wide_ref[...], 0, 0)).astype(BF16)
    width = low_ref.shape[1]
    for a in range(local):
        out_ref[a] = out[:, a * width : (a + 1) * width]


def shards(tokens, tenant, send_list, base_weight, down_weight, up_weight, cotangent):
    rows, width = tokens.shape
    span = cotangent.shape[1]
    local, _, pair = down_weight.shape
    rank = up_weight.shape[1]
    holders, capacity = send_list.shape[1], send_list.shape[2]
    slots = holders * capacity
    fsdp = lax.axis_size("fsdp")
    upper, odd_place = call(place_body, "place", [shape((1, 1), F32)] * 2, [], vmem=1)

    def where(mask, yes, no):
        mask = jnp.broadcast_to(mask, yes.shape)
        return jnp.where(mask > 0.5, yes, no)
    half = rows // 2
    chunk = 512

    (message,) = call(
        lambda *refs: message_body(local, *refs),
        "message",
        [shape((rows + 16, span))],
        [pltpu.with_memory_space_constraint(a, pltpu.HBM) for a in (cotangent, send_list, tenant.reshape(-1, capacity))],
        grid=(1,),
        in_specs=[
            pl.BlockSpec(cotangent.shape, lambda i: (0, 0)),
            pl.BlockSpec(send_list.shape, lambda i: (0, 0, 0)),
            pl.BlockSpec((rows // capacity, capacity), lambda i: (0, 0)),
        ],
        out_specs=[pl.BlockSpec((rows + 16, span), lambda i: (0, 0))],
    )
    near = {0: message}
    for bits in (2, 4, 6):
        near[bits] = swap(message, "adapter", bits)
    top, bottom = tokens[:half], tokens[half:]
    base_partial = jnp.dot(tokens, base_weight, preferred_element_type=F32).astype(BF16)
    near[2], near[4], near[6], top = tie((near[2], near[4], near[6], top), (base_partial,))
    messages = []
    for bits in ORDER[::2]:
        messages += [near[bits], swap(near[bits], "adapter", 1)]
    slots_dy, ids, own, mate, back_part = call(
        lambda *refs: back_body(holders, capacity, rank, local, *refs),
        "back_rows",
        [
            shape((holders, capacity, span)),
            shape((holders, capacity, capacity), F32),
            shape((holders, rows, capacity)),
            shape((holders // 2, rows, capacity)),
            shape((holders // 2, capacity, 2 * rank), F32),
        ],
        [*messages, up_weight],
    )
    back_part = back_part.reshape(slots // 2, 2 * rank)
    flat_ids = ids.reshape(slots, capacity)

    def low_rows(first, blocks, needs=()):
        count = len(blocks)
        pieces = sum(blocks, ())
        starts = [p[1] * half if isinstance(p, tuple) else 0 for p in pieces]
        return call(
            lambda *refs: low_body(local, count, first, starts, *refs),
            "low_rows",
            [shape((count * capacity, width)), shape((count * capacity, pair), F32)],
            [p[0] if isinstance(p, tuple) else p for p in pieces] + [own, ids, down_weight],
            vmem=16,
            needs=needs,
        )

    def with_mates(*blocks):
        out = []
        for block in blocks:
            out += [block, tuple(swap(piece, "adapter", 1) for piece in block)]
        return out

    got1 = swap(back_part.astype(BF16), "fsdp", 1)
    x_top, y_top = swap(top, "adapter", 2), swap(top, "adapter", 4)
    x_a, low_a = low_rows(0, with_mates((tokens,)))
    back_half = (back_part + got1.astype(F32)).astype(BF16)
    (back_half,) = tie((back_half,), (x_top, y_top, low_a))
    (base_partial,) = tie((base_partial,), (got1,))

    back_other = swap(back_half, "fsdp", 2)
    x_bottom, y_bottom = swap(bottom, "adapter", 2), swap(bottom, "adapter", 4)
    top_mates = swap(jnp.concatenate([y_top, x_top], axis=0), "adapter", 1)
    quarter = [base_partial[:, i * span : (i + 1) * span] for i in range(4)]
    base_keep = [where(odd_place, quarter[1], quarter[0]), where(odd_place, quarter[3], quarter[2])]
    base_give = [where(odd_place, quarter[0], quarter[1]), where(odd_place, quarter[2], quarter[3])]
    base_got = swap(jnp.concatenate(base_give, axis=1), "fsdp", 1)
    lower_half, upper_half = where(upper, back_other, back_half), where(upper, back_half, back_other)
    back_low = jnp.concatenate(
        [
            jnp.concatenate([lower_half[:, i : i + rank], upper_half[:, i : i + rank]], axis=1)
            for i in (0, rank)
        ],
        axis=0,
    )

    def back_delta(part, needs):
        (out,) = call(
            lambda *refs: delta_body(local, part, *refs),
            "back_delta",
            [shape((holders // 2, capacity, width))],
            [back_low, ids, down_weight],
            grid=(width // chunk,),
            in_specs=[
                pl.BlockSpec((slots, pair), lambda i: (0, 0)),
                pl.BlockSpec((holders, capacity, capacity), lambda i: (0, 0, 0)),
                pl.BlockSpec((local, chunk, pair), lambda i: (0, i, 0)),
            ],
            out_specs=[pl.BlockSpec((holders // 2, capacity, chunk), lambda i: (0, 0, i))],
            scratch=[pltpu.VMEM((slots // 2, local * pair), BF16)],
            vmem=16,
            needs=needs,
        )
        return out

    odd = back_delta(1, (x_bottom, y_bottom, top_mates, base_got))
    even = back_delta(0, (odd,))

    got = swap(odd, "adapter", 1)
    diag = (swap(y_top, "adapter", 2), swap(x_bottom, "adapter", 4))
    far_dy = swap(cotangent, "fsdp", 2)
    bottom_mates = swap(jnp.concatenate([y_bottom, x_bottom], axis=0), "adapter", 1)
    x_b, low_b = low_rows(
        4,
        [
            (y_top, y_bottom),
            ((top_mates, 0), (bottom_mates, 0)),
            (x_top, x_bottom),
            ((top_mates, 1), (bottom_mates, 1)),
        ],
    )
    diag_low, diag_high = expand(
        "back_diag", 1, 1, ((0, 0, half), (0, half, half)), own, mate, even, got, 1024
    )
    y_low, y_high, x_low, x_high = expand(
        "back_near",
        2,
        2,
        ((0, 0, half), (0, half, half), (1, 0, half), (1, half, half)),
        own,
        mate,
        even,
        got,
        1024,
    )
    *diag, far_dy = tie((*diag, far_dy), (low_b, diag_low, y_low))

    low_in = swap(diag_low, "adapter", 2)
    high_in = swap(diag_high, "adapter", 4)
    x_c, low_c = low_rows(2, with_mates(tuple(diag)))
    low_part = jnp.concatenate([low_a, low_c, low_b], axis=0)
    halves = [
        jnp.concatenate([low_part[: slots // 2, i : i + rank], low_part[slots // 2 :, i : i + rank]], axis=1)
        for i in (0, rank)
    ]
    keep, give = where(upper, halves[1], halves[0]), where(upper, halves[0], halves[1]).astype(BF16)
    to_y, to_x = y_low + low_in, x_high + high_in
    got_low = swap(give, "fsdp", 2)
    next_dy = swap(jnp.stack([cotangent, far_dy]), "fsdp", 1)
    down_grad, made = call(
        lambda *refs: down_grad_body(local, 3, *refs),
        "down_grad",
        [shape((local, width, pair)), shape((8, 128), F32)],
        [x_a, x_c, x_b, back_low, flat_ids],
        grid=(width // 256,),
        in_specs=[pl.BlockSpec((x.shape[0], 256), lambda i: (0, i)) for x in (x_a, x_c, x_b)]
        + [pl.BlockSpec((slots, pair), lambda i: (0, 0)), pl.BlockSpec((slots, capacity), lambda i: (0, 0))],
        out_specs=[pl.BlockSpec((local, 256, pair), lambda i: (0, i, 0)), pl.BlockSpec((8, 128), lambda i: (0, 0))],
        scratch=[pltpu.VMEM((slots, local * pair), BF16)],
        vmem=16,
    )
    low_sum = keep + got_low.astype(F32)
    low_sent, base_got, y_high, x_low = tie(
        (low_sum.astype(BF16), base_got, y_high, x_low), (to_y, to_x, next_dy)
    )

    got2 = swap(low_sent, "fsdp", 1)
    high_from_y = swap(y_high, "adapter", 4)
    low_from_x = swap(x_low, "adapter", 2)
    ordered = [
        where(odd_place, b, a) for a, b in ((cotangent, next_dy[0]), (next_dy[0], cotangent))
    ], [where(odd_place, b, a) for a, b in ((far_dy, next_dy[1]), (next_dy[1], far_dy))]
    all_dy = jnp.concatenate(
        [where(upper, ordered[1 - i][j], ordered[i][j]) for i in range(2) for j in range(2)], axis=1
    )
    input_base = contract(all_dy, base_weight, 1, 1)
    (home,) = expand("back_home", 0, 1, ((0, 0, rows),), own, mate, even, got, 1024)
    base_sum = [
        base_keep[i].astype(F32) + base_got[:, i * span : (i + 1) * span].astype(F32) for i in range(2)
    ]
    base_far = swap(where(upper, base_sum[0], base_sum[1]).astype(BF16), "fsdp", 2)
    base_out = where(upper, base_sum[1], base_sum[0]) + base_far.astype(F32)
    low_half = (low_sum + got2.astype(F32)).astype(BF16)
    up_odd, up_even, wide_low, to_y, to_x, input_base = call(
        lambda *refs: up_body(local, *refs),
        "up_delta",
        [shape((holders // 2, capacity, span))] * 2 + [shape((slots, local * rank))],
        [low_half, ids, up_weight],
        needs=(home, high_from_y, low_from_x, base_far, made),
        passed=(to_y, to_x, input_base),
    )

    low_from_y = swap(to_y, "adapter", 4)
    high_from_x = swap(to_x, "adapter", 2)
    up_got = swap(up_odd, "adapter", 1)
    add_home, add_diag, add_y, add_x = expand(
        "up_rows", 0, 4, tuple((p, 0, rows) for p in range(4)), own, mate, up_even, up_got, 512
    )
    add_x = swap(add_x, "adapter", 2)
    add_y = swap(add_y, "adapter", 4)
    add_diag = swap(add_diag, "adapter", 6)
    up_grad = adapter_scale * contract(wide_low, slots_dy.reshape(slots, span), 0, 0)
    up_grad = up_grad.astype(BF16).reshape(local, rank, span)

    projected = (base_out + (add_home + add_x + add_y + add_diag).astype(F32)).astype(BF16)
    low_rows_out = home[:half] + low_from_x + low_from_y
    high_rows_out = home[half:] + high_from_x + high_from_y
    token_gradient = (
        input_base + jnp.concatenate([low_rows_out, high_rows_out], axis=0).astype(F32)
    ).astype(BF16)
    return (projected, token_gradient, down_grad, up_grad)


def solution(mesh):
    in_specs = (
        P("adapter", "fsdp"),
        P("adapter"),
        P("adapter", None, None),
        P("fsdp", None),
        P("adapter", "fsdp", None),
        P("adapter", None, "fsdp"),
        P("adapter", "fsdp"),
    )
    out_specs = (
        P("adapter", "fsdp"),
        P("adapter", "fsdp"),
        P("adapter", "fsdp", None),
        P("adapter", None, "fsdp"),
    )
    program = shards if mesh.shape["adapter"] == 8 and mesh.shape["fsdp"] == 4 else shards_any
    return jax.shard_map(program, mesh=mesh, in_specs=in_specs, out_specs=out_specs, check_vma=False)
```

```python
import jax
import jax.numpy as jnp
from jax import lax
from jax.experimental import pallas as pl
from jax.experimental.pallas import tpu as pltpu
from jax.sharding import PartitionSpec as P

KV = 1024


adapter_scale = 0.5


def down_partial(input_rows, weights_f, down_weight):
    low_all = jnp.einsum("sd,ldk->slk", input_rows, down_weight, preferred_element_type=jnp.float32)
    return jnp.sum(low_all * weights_f[:, :, None], axis=1)


def grad_partial(rows_dy, weights_f, up_projection_weight, selected_half):
    rank_size = up_projection_weight.shape[1]
    back_all = jnp.einsum(
        "sc,lrc->slr", rows_dy, up_projection_weight, preferred_element_type=jnp.float32
    )
    half_sum = jnp.sum(back_all * weights_f[:, :, None], axis=1)
    placed = jnp.zeros((rows_dy.shape[0], 2 * rank_size), jnp.float32)
    zero_idx = jnp.zeros((), jnp.int32)
    return lax.dynamic_update_slice(placed, half_sum, (zero_idx, selected_half * rank_size))


def forward_holder(low_rank, weight_table, up_projection_weight, selected_half):
    rank_size = up_projection_weight.shape[1]
    low_half = lax.dynamic_slice_in_dim(low_rank, selected_half * rank_size, rank_size, 1)
    broadcast_rows = low_half[:, None, :] * weight_table[:, :, None]
    adapter_update = adapter_scale * jnp.einsum(
        "slr,lrc->sc", broadcast_rows, up_projection_weight, preferred_element_type=jnp.float32
    )
    return (adapter_update.astype(jnp.bfloat16), broadcast_rows)


def backward_owner(back_low, weight_table, input_rows, rows_dy, broadcast_rows, down_weight):
    widened_rows = back_low[:, None, :] * weight_table[:, :, None]
    backward_update = adapter_scale * jnp.einsum(
        "wnr,nyr->wy", widened_rows, down_weight, preferred_element_type=jnp.float32
    )
    down_weight_gradient = adapter_scale * jnp.einsum(
        "wq,wmu->mqu", input_rows, widened_rows, preferred_element_type=jnp.float32
    )
    up_weight_gradient = adapter_scale * jnp.einsum(
        "slr,sc->lrc", broadcast_rows, rows_dy, preferred_element_type=jnp.float32
    )
    return (
        backward_update.astype(jnp.bfloat16),
        down_weight_gradient.astype(jnp.bfloat16),
        up_weight_gradient.astype(jnp.bfloat16),
    )


def shards_any(tokens, tenant, send_list, base_weight, down_weight, up_projection_weight, cotangent):
    rows_here = tokens.shape[0]
    width_here = tokens.shape[1]
    column_span = cotangent.shape[1]
    adapters_here = down_weight.shape[0]
    holder_list = send_list.shape[1]
    slot_capacity = send_list.shape[2]
    total_slots = holder_list * slot_capacity
    listed = send_list[0]
    present = listed >= 0
    safe_rows = jnp.where(present, listed, 0)
    local_ids = tenant % adapters_here
    picked_ids = local_ids[safe_rows]
    adapter_ids = jnp.arange(adapters_here, dtype=jnp.int32)
    selector = (
        (picked_ids[:, :, None] == adapter_ids[None, None, :]) & present[:, :, None]
    ).astype(jnp.bfloat16)
    send_x = tokens[safe_rows]
    send_dy = cotangent[safe_rows]
    drop_rows = jnp.where(present, listed, rows_here).reshape(total_slots)
    fsdp_pos = lax.axis_index("fsdp")
    selected_half = fsdp_pos * column_span // KV
    weight_cols = base_weight
    local_base_output = lax.psum_scatter(
        lax.dot_general(
            weight_cols, tokens, (((0,), (1,)), ((), ())), preferred_element_type=jnp.float32
        ),
        "fsdp",
        scatter_dimension=0,
        tiled=True,
    ).T
    weight_cols = base_weight
    input_frozen_part = lax.dot_general(
        lax.all_gather(cotangent, "fsdp", axis=1, tiled=True),
        weight_cols,
        (((1,), (1,)), ((), ())),
        preferred_element_type=jnp.float32,
    )
    recv_x, recv_sel = (
        lax.all_to_all(send_x, "adapter", split_axis=0, concat_axis=0, tiled=True),
        lax.all_to_all(selector, "adapter", split_axis=0, concat_axis=0, tiled=True),
    )
    input_rows = recv_x.reshape(total_slots, width_here)
    weight_table = recv_sel.reshape(total_slots, adapters_here)
    weights_f = weight_table.astype(jnp.float32)
    low_term = down_partial(input_rows, weights_f, down_weight)
    reduced_rank_sum = lax.psum(low_term, "fsdp")
    adapter_update, broadcast_rows = forward_holder(
        reduced_rank_sum.astype(jnp.bfloat16), weight_table, up_projection_weight, selected_half
    )
    got_delta = lax.all_to_all(
        adapter_update.reshape(holder_list, slot_capacity, column_span),
        "adapter",
        split_axis=0,
        concat_axis=0,
        tiled=True,
    )
    recv_dy = lax.all_to_all(send_dy, "adapter", split_axis=0, concat_axis=0, tiled=True)
    rows_dy = recv_dy.reshape(total_slots, column_span)
    back_sum = lax.psum(
        grad_partial(rows_dy, weights_f, up_projection_weight, selected_half), "fsdp"
    )
    backward_update, down_weight_gradient, up_weight_gradient = backward_owner(
        back_sum.astype(jnp.bfloat16),
        weight_table,
        input_rows,
        rows_dy,
        broadcast_rows,
        down_weight,
    )
    got_back = lax.all_to_all(
        backward_update.reshape(holder_list, slot_capacity, width_here),
        "adapter",
        split_axis=0,
        concat_axis=0,
        tiled=True,
    )
    adapter_columns = (
        jnp.zeros((rows_here, column_span), jnp.float32)
        .at[drop_rows]
        .add(got_delta.reshape(total_slots, column_span).astype(jnp.float32), mode="drop")
    )
    projected = (local_base_output + adapter_columns).astype(jnp.bfloat16)
    adapter_backward = (
        jnp.zeros((rows_here, width_here), jnp.float32)
        .at[drop_rows]
        .add(got_back.reshape(total_slots, width_here).astype(jnp.float32), mode="drop")
    )
    token_gradient = (input_frozen_part + adapter_backward).astype(jnp.bfloat16)
    return (projected, token_gradient, down_weight_gradient, up_weight_gradient)

BF16 = jnp.bfloat16
F32 = jnp.float32
MIB = 1 << 20
HINT_FLOPS, HINT_BYTES = 1 << 10, 1 << 10


def contract(left, right, left_dim, right_dim):
    return lax.dot_general(
        left, right, (((left_dim,), (right_dim,)), ((), ())), preferred_element_type=F32
    )


def swap(value, axis, bits):
    size = lax.axis_size(axis)
    return lax.ppermute(value, axis, [(i, i ^ bits) for i in range(size)])


def call(body, name, outs, args, *, grid=(), in_specs=None, out_specs=None, scratch=(), scalars=0, vmem=12, needs=(), passed=(), hint=1):
    given = len(args)
    extra = [*needs, *passed]
    in_specs = list(in_specs) if in_specs is not None else [pl.BlockSpec()] * (given - scalars)
    out_specs = list(out_specs) if out_specs is not None else [pl.BlockSpec()] * len(outs)
    anywhere = pl.BlockSpec(memory_space=pl.ANY)
    count = len(outs)
    outs = [*outs, *(shape(p.shape, p.dtype) for p in passed)]
    out_specs += [anywhere] * len(passed)
    aliases = {given + len(needs) + i: count + i for i in range(len(passed))}

    def run(*refs):
        kept = refs[:given] + refs[given + len(extra) : given + len(extra) + count]
        body(*kept, *refs[given + len(extra) + len(outs) :])

    spec = pltpu.PrefetchScalarGridSpec(
        num_scalar_prefetch=scalars,
        grid=grid,
        in_specs=in_specs + [anywhere] * len(extra),
        out_specs=out_specs,
        scratch_shapes=list(scratch),
    )
    return pl.pallas_call(
        run,
        grid_spec=spec,
        out_shape=outs,
        name=name,
        input_output_aliases=aliases,
        cost_estimate=pl.CostEstimate(
            flops=HINT_FLOPS * hint, bytes_accessed=HINT_BYTES * hint, transcendentals=0
        ),
        compiler_params=pltpu.CompilerParams(vmem_limit_bytes=vmem * MIB),
    )(*args, *extra)


def tie(values, needs):
    count, total = len(values), len(values) + len(needs)
    anywhere = pl.BlockSpec(memory_space=pl.ANY)
    return pl.pallas_call(
        lambda *refs: None,
        in_specs=[anywhere] * total,
        out_specs=[anywhere] * count,
        out_shape=[shape(v.shape, v.dtype) for v in values],
        name="tie",
        input_output_aliases={i: i for i in range(count)},
        cost_estimate=pl.CostEstimate(flops=HINT_FLOPS, bytes_accessed=HINT_BYTES, transcendentals=0),
        compiler_params=pltpu.CompilerParams(vmem_limit_bytes=MIB),
    )(*values, *needs)


def shape(dims, dtype=BF16):
    return jax.ShapeDtypeStruct(dims, dtype)


ORDER = (0, 1, 6, 7, 4, 5, 2, 3)


def after(value, *others):
    return lax.optimization_barrier((value, *others))[0]


def back_body(holders, capacity, rank, local, *refs):
    messages, up_ref = refs[:holders], refs[holders]
    dy_ref, ids_ref, own_ref, mate_ref, part_ref = refs[holders + 1 :]
    me = lax.axis_index("adapter")
    rows = messages[0].shape[0] - 16
    span = up_ref.shape[2]
    owner = lax.broadcasted_iota(jnp.int32, (holders, capacity), 0)
    row_id = lax.broadcasted_iota(jnp.int32, (rows, capacity), 0).astype(F32)
    upper_lanes = (lax.broadcasted_iota(jnp.int32, (capacity, 2 * rank), 1) >= rank).astype(F32)
    up = up_ref[...].reshape(local * rank, span)
    parts = []
    for g in range(holders):
        tail = messages[g][rows : rows + 16, :capacity].astype(F32)
        lists, ids = tail[:holders], tail[holders:]
        listed = jnp.sum(jnp.where(owner == me, lists, 0.0), axis=0, keepdims=True)
        pick = (row_id == listed).astype(F32).astype(BF16)
        own_ref[g] = pick
        if g % 2 == 0:
            other = jnp.sum(jnp.where(owner == (me ^ 1), lists, 0.0), axis=0, keepdims=True)
            mate_ref[g // 2] = (row_id == other).astype(F32).astype(BF16)
        column = ids.T
        adapter = jnp.concatenate([column[:, j : j + 1] for j in range(rows // capacity)], axis=0)
        adapter = jnp.broadcast_to(adapter + 1.0, (rows, capacity)).astype(BF16)
        ids = contract(pick, adapter, 0, 0)
        ids_ref[g] = ids
        dy = contract(pick, messages[g][:rows, :], 0, 0).astype(BF16)
        dy_ref[g] = dy
        wide = contract(dy, up, 1, 1)
        total = jnp.zeros((capacity, 2 * rank), F32)
        for p in range(local // 2):
            wanted = upper_lanes + (2 * p + 1.0)
            total += jnp.where(ids == wanted, wide[:, 2 * rank * p : 2 * rank * (p + 1)], 0.0)
        parts.append(total[:, :rank] + total[:, rank:])
    for g in range(holders // 2):
        part_ref[g] = jnp.concatenate([parts[g], parts[g + holders // 2]], axis=1)


def message_body(local, dy_ref, lists_ref, tenant_ref, out_ref):
    rows, span = dy_ref.shape
    _, holders, capacity = lists_ref.shape
    count = tenant_ref.shape[0]
    out_ref[:rows, :] = dy_ref[...]
    ids = lax.rem(tenant_ref[...], local).astype(F32)
    tail = jnp.concatenate([lists_ref[0].astype(F32), ids, jnp.zeros((16 - holders - count, capacity), F32)], axis=0)
    tail = jnp.concatenate([tail, jnp.zeros((16, span - capacity), F32)], axis=1)
    out_ref[rows:, :] = tail.astype(BF16)


def place_body(upper_ref, odd_ref):
    place = lax.axis_index("fsdp")
    upper_ref[...] = jnp.full(upper_ref.shape, (place >= lax.axis_size("fsdp") // 2).astype(F32))
    odd_ref[...] = jnp.full(odd_ref.shape, (place & 1).astype(F32))


def low_body(local, count, first, starts, *refs):
    own_ref, ids_ref, down_ref, slots_ref, part_ref = refs[-5:]
    pieces = (len(refs) - 5) // count
    rows = own_ref.shape[1] // pieces
    capacity = own_ref.shape[2]
    width = down_ref.shape[2]
    for j in range(count):
        picked = 0.0
        for i in range(pieces):
            at = starts[pieces * j + i]
            piece = refs[pieces * j + i][at : at + rows, :]
            picked += contract(own_ref[first + j, i * rows : (i + 1) * rows], piece, 0, 0)
        slots_ref[j * capacity : (j + 1) * capacity, :] = picked.astype(BF16)
    ids = ids_ref[first : first + count].reshape(count * capacity, capacity)
    total = jnp.zeros((count * capacity, width), F32)
    for a in range(0, local, 2):
        weights = jnp.concatenate([down_ref[a], down_ref[a + 1]], axis=1)
        wide = contract(slots_ref[...], weights, 1, 0)
        total += jnp.where(ids == a + 1.0, wide[:, :width], 0.0)
        total += jnp.where(ids == a + 2.0, wide[:, width:], 0.0)
    part_ref[...] = total


def spread(low, ids, local):
    low = low.astype(F32)
    return jnp.concatenate([jnp.where(ids == a + 1.0, low, 0.0) for a in range(local)], axis=1).astype(BF16)


def delta_body(local, part, low_ref, ids_ref, down_ref, out_ref, wide_ref):
    holders, capacity, _ = ids_ref.shape

    @pl.when(pl.program_id(0) == 0)
    def _():
        for i, g in enumerate(range(part, holders, 2)):
            wide_ref[i * capacity : (i + 1) * capacity, :] = spread(
                low_ref[g * capacity : (g + 1) * capacity, :], ids_ref[g], local
            )

    weights = jnp.concatenate([down_ref[a] for a in range(local)], axis=1)
    out = (adapter_scale * contract(wide_ref[...], weights, 1, 1)).astype(BF16)
    out_ref[...] = out.reshape(out_ref.shape)


def up_body(local, low_ref, ids_ref, up_ref, odd_ref, even_ref, wide_ref):
    slots, rank = 2 * low_ref.shape[0], low_ref.shape[1] // 2
    holders, capacity, _ = ids_ref.shape
    packed = low_ref[...].astype(F32)
    low = jnp.concatenate(
        [jnp.concatenate([packed[:, i : i + rank]] * 2, axis=1) for i in (0, rank)], axis=0
    )
    ids = ids_ref[...].reshape(slots, capacity)
    upper_lanes = (lax.broadcasted_iota(jnp.int32, (slots, 2 * rank), 1) >= rank).astype(F32)
    wide = jnp.concatenate(
        [jnp.where(ids == upper_lanes + (2 * p + 1.0), low, 0.0) for p in range(local // 2)], axis=1
    ).astype(BF16)
    wide_ref[...] = wide
    span = up_ref.shape[2]
    up = up_ref[...].reshape(local * rank, span)
    out = (adapter_scale * contract(wide, up, 1, 0)).astype(BF16)
    for g in range(holders):
        (odd_ref if g % 2 else even_ref)[g // 2] = out[g * capacity : (g + 1) * capacity]


def expand_body(picks, own_ref, mate_ref, even_ref, got_ref, *out_refs):
    for (p, first, count), out_ref in zip(picks, out_refs):
        pick = jnp.concatenate(
            [own_ref[2 * p][first : first + count], mate_ref[p][first : first + count]], axis=1
        )
        both = jnp.concatenate([even_ref[p], got_ref[p]], axis=0)
        out_ref[...] = contract(pick, both, 1, 0).astype(BF16)


def expand(name, start, pairs, picks, own, mate, even, got, step, needs=()):
    rows, capacity = own.shape[1:]
    width = even.shape[2]
    step = min(width, step)
    block = start // pairs
    return call(
        lambda *refs: expand_body(picks, *refs),
        name,
        [shape((count, width)) for _, _, count in picks],
        [own, mate, even, got],
        grid=(width // step,),
        in_specs=[
            pl.BlockSpec((2 * pairs, rows, capacity), lambda i: (block, 0, 0)),
            pl.BlockSpec((pairs, rows, capacity), lambda i: (block, 0, 0)),
            pl.BlockSpec((pairs, capacity, step), lambda i: (block, 0, i)),
            pl.BlockSpec((pairs, capacity, step), lambda i: (block, 0, i)),
        ],
        out_specs=[pl.BlockSpec((count, step), lambda i: (0, i)) for _, _, count in picks],
        needs=needs,
    )


def down_grad_body(local, pieces, *refs):
    blocks = refs[:pieces]
    low_ref, ids_ref, out_ref, made_ref, wide_ref = refs[pieces:]
    made_ref[...] = jnp.zeros_like(made_ref)
    slots = low_ref.shape[0]

    @pl.when(pl.program_id(0) == 0)
    def _():
        wide_ref[...] = spread(low_ref[...], ids_ref[...].reshape(slots, -1), local)

    rows = jnp.concatenate([block[...] for block in blocks], axis=0)
    out = (adapter_scale * contract(rows, wide_ref[...], 0, 0)).astype(BF16)
    width = low_ref.shape[1]
    for a in range(local):
        out_ref[a] = out[:, a * width : (a + 1) * width]


def shards(tokens, tenant, send_list, base_weight, down_weight, up_weight, cotangent):
    rows, width = tokens.shape
    span = cotangent.shape[1]
    local, _, pair = down_weight.shape
    rank = up_weight.shape[1]
    holders, capacity = send_list.shape[1], send_list.shape[2]
    slots = holders * capacity
    fsdp = lax.axis_size("fsdp")
    upper, odd_place = call(place_body, "place", [shape((1, 1), F32)] * 2, [], vmem=1)

    def where(mask, yes, no):
        mask = jnp.broadcast_to(mask, yes.shape)
        return jnp.where(mask > 0.5, yes, no)
    half = rows // 2
    chunk = 512

    (message,) = call(
        lambda *refs: message_body(local, *refs),
        "message",
        [shape((rows + 16, span))],
        [pltpu.with_memory_space_constraint(a, pltpu.HBM) for a in (cotangent, send_list, tenant.reshape(-1, capacity))],
        grid=(1,),
        in_specs=[
            pl.BlockSpec(cotangent.shape, lambda i: (0, 0)),
            pl.BlockSpec(send_list.shape, lambda i: (0, 0, 0)),
            pl.BlockSpec((rows // capacity, capacity), lambda i: (0, 0)),
        ],
        out_specs=[pl.BlockSpec((rows + 16, span), lambda i: (0, 0))],
    )
    near = {0: message}
    for bits in (2, 4, 6):
        near[bits] = swap(message, "adapter", bits)
    top, bottom = tokens[:half], tokens[half:]
    base_partial = jnp.dot(tokens, base_weight, preferred_element_type=F32).astype(BF16)
    near[2], near[4], near[6], top = tie((near[2], near[4], near[6], top), (base_partial,))
    messages = []
    for bits in ORDER[::2]:
        messages += [near[bits], swap(near[bits], "adapter", 1)]
    slots_dy, ids, own, mate, back_part = call(
        lambda *refs: back_body(holders, capacity, rank, local, *refs),
        "back_rows",
        [
            shape((holders, capacity, span)),
            shape((holders, capacity, capacity), F32),
            shape((holders, rows, capacity)),
            shape((holders // 2, rows, capacity)),
            shape((holders // 2, capacity, 2 * rank), F32),
        ],
        [*messages, up_weight],
    )
    back_part = back_part.reshape(slots // 2, 2 * rank)
    flat_ids = ids.reshape(slots, capacity)

    def low_rows(first, blocks, needs=()):
        count = len(blocks)
        pieces = sum(blocks, ())
        starts = [p[1] * half if isinstance(p, tuple) else 0 for p in pieces]
        return call(
            lambda *refs: low_body(local, count, first, starts, *refs),
            "low_rows",
            [shape((count * capacity, width)), shape((count * capacity, pair), F32)],
            [p[0] if isinstance(p, tuple) else p for p in pieces] + [own, ids, down_weight],
            vmem=16,
            needs=needs,
        )

    def with_mates(*blocks):
        out = []
        for block in blocks:
            out += [block, tuple(swap(piece, "adapter", 1) for piece in block)]
        return out

    got1 = swap(back_part.astype(BF16), "fsdp", 1)
    x_top, y_top = swap(top, "adapter", 2), swap(top, "adapter", 4)
    x_a, low_a = low_rows(0, with_mates((tokens,)))
    back_half = (back_part + got1.astype(F32)).astype(BF16)
    (back_half,) = tie((back_half,), (x_top, y_top, low_a))
    base_partial, bottom = tie((base_partial, bottom), (got1,))

    back_other = swap(back_half, "fsdp", 2)
    x_bottom, y_bottom = swap(bottom, "adapter", 2), swap(bottom, "adapter", 4)
    top_mates = swap(jnp.concatenate([y_top, x_top], axis=0), "adapter", 1)
    quarter = [base_partial[:, i * span : (i + 1) * span] for i in range(4)]
    base_keep = [where(odd_place, quarter[1], quarter[0]), where(odd_place, quarter[3], quarter[2])]
    base_give = [where(odd_place, quarter[0], quarter[1]), where(odd_place, quarter[2], quarter[3])]
    base_got = swap(jnp.concatenate(base_give, axis=1), "fsdp", 1)
    lower_half, upper_half = where(upper, back_other, back_half), where(upper, back_half, back_other)
    back_low = jnp.concatenate(
        [
            jnp.concatenate([lower_half[:, i : i + rank], upper_half[:, i : i + rank]], axis=1)
            for i in (0, rank)
        ],
        axis=0,
    )

    def back_delta(part, needs):
        (out,) = call(
            lambda *refs: delta_body(local, part, *refs),
            "back_delta",
            [shape((holders // 2, capacity, width))],
            [back_low, ids, down_weight],
            grid=(width // chunk,),
            in_specs=[
                pl.BlockSpec((slots, pair), lambda i: (0, 0)),
                pl.BlockSpec((holders, capacity, capacity), lambda i: (0, 0, 0)),
                pl.BlockSpec((local, chunk, pair), lambda i: (0, i, 0)),
            ],
            out_specs=[pl.BlockSpec((holders // 2, capacity, chunk), lambda i: (0, 0, i))],
            scratch=[pltpu.VMEM((slots // 2, local * pair), BF16)],
            vmem=16,
            needs=needs,
        )
        return out

    odd = back_delta(1, (x_bottom, y_bottom, top_mates, base_got))
    even = back_delta(0, (odd,))

    got = swap(odd, "adapter", 1)
    diag = (swap(y_top, "adapter", 2), swap(x_bottom, "adapter", 4))
    far_dy = swap(cotangent, "fsdp", 2)
    bottom_mates = swap(jnp.concatenate([y_bottom, x_bottom], axis=0), "adapter", 1)
    x_b, low_b = low_rows(
        4,
        [
            (y_top, y_bottom),
            ((top_mates, 0), (bottom_mates, 0)),
            (x_top, x_bottom),
            ((top_mates, 1), (bottom_mates, 1)),
        ],
    )
    diag_low, diag_high = expand(
        "back_diag", 1, 1, ((0, 0, half), (0, half, half)), own, mate, even, got, 1024
    )
    y_low, y_high, x_low, x_high = expand(
        "back_near",
        2,
        2,
        ((0, 0, half), (0, half, half), (1, 0, half), (1, half, half)),
        own,
        mate,
        even,
        got,
        1024,
    )
    *diag, far_dy = tie((*diag, far_dy), (low_b, diag_low, y_low))

    low_in = swap(diag_low, "adapter", 2)
    high_in = swap(diag_high, "adapter", 4)
    x_c, low_c = low_rows(2, with_mates(tuple(diag)))
    low_part = jnp.concatenate([low_a, low_c, low_b], axis=0)
    halves = [
        jnp.concatenate([low_part[: slots // 2, i : i + rank], low_part[slots // 2 :, i : i + rank]], axis=1)
        for i in (0, rank)
    ]
    keep, give = where(upper, halves[1], halves[0]), where(upper, halves[0], halves[1]).astype(BF16)
    to_y, to_x = y_low + low_in, x_high + high_in
    got_low = swap(give, "fsdp", 2)
    next_dy = swap(jnp.stack([cotangent, far_dy]), "fsdp", 1)
    down_grad, made = call(
        lambda *refs: down_grad_body(local, 3, *refs),
        "down_grad",
        [shape((local, width, pair)), shape((8, 128), F32)],
        [x_a, x_c, x_b, back_low, flat_ids],
        grid=(width // 256,),
        in_specs=[pl.BlockSpec((x.shape[0], 256), lambda i: (0, i)) for x in (x_a, x_c, x_b)]
        + [pl.BlockSpec((slots, pair), lambda i: (0, 0)), pl.BlockSpec((slots, capacity), lambda i: (0, 0))],
        out_specs=[pl.BlockSpec((local, 256, pair), lambda i: (0, i, 0)), pl.BlockSpec((8, 128), lambda i: (0, 0))],
        scratch=[pltpu.VMEM((slots, local * pair), BF16)],
        vmem=16,
    )
    low_sum = keep + got_low.astype(F32)
    low_sent, base_got, y_high, x_low = tie(
        (low_sum.astype(BF16), base_got, y_high, x_low), (to_y, to_x, next_dy)
    )

    got2 = swap(low_sent, "fsdp", 1)
    high_from_y = swap(y_high, "adapter", 4)
    low_from_x = swap(x_low, "adapter", 2)
    ordered = [
        where(odd_place, b, a) for a, b in ((cotangent, next_dy[0]), (next_dy[0], cotangent))
    ], [where(odd_place, b, a) for a, b in ((far_dy, next_dy[1]), (next_dy[1], far_dy))]
    all_dy = jnp.concatenate(
        [where(upper, ordered[1 - i][j], ordered[i][j]) for i in range(2) for j in range(2)], axis=1
    )
    input_base = contract(all_dy, base_weight, 1, 1)
    (home,) = expand("back_home", 0, 1, ((0, 0, rows),), own, mate, even, got, 1024)
    base_sum = [
        base_keep[i].astype(F32) + base_got[:, i * span : (i + 1) * span].astype(F32) for i in range(2)
    ]
    base_far = swap(where(upper, base_sum[0], base_sum[1]).astype(BF16), "fsdp", 2)
    base_out = where(upper, base_sum[1], base_sum[0]) + base_far.astype(F32)
    low_half = (low_sum + got2.astype(F32)).astype(BF16)
    up_odd, up_even, wide_low, to_y, to_x, input_base = call(
        lambda *refs: up_body(local, *refs),
        "up_delta",
        [shape((holders // 2, capacity, span))] * 2 + [shape((slots, local * rank))],
        [low_half, ids, up_weight],
        needs=(home, high_from_y, low_from_x, base_far, made),
        passed=(to_y, to_x, input_base),
    )

    low_from_y = swap(to_y, "adapter", 4)
    high_from_x = swap(to_x, "adapter", 2)
    up_got = swap(up_odd, "adapter", 1)
    add_home, add_diag, add_y, add_x = expand(
        "up_rows", 0, 4, tuple((p, 0, rows) for p in range(4)), own, mate, up_even, up_got, 512
    )
    add_x = swap(add_x, "adapter", 2)
    add_y = swap(add_y, "adapter", 4)
    add_diag = swap(add_diag, "adapter", 6)
    up_grad = adapter_scale * contract(wide_low, slots_dy.reshape(slots, span), 0, 0)
    up_grad = up_grad.astype(BF16).reshape(local, rank, span)

    projected = (base_out + (add_home + add_x + add_y + add_diag).astype(F32)).astype(BF16)
    low_rows_out = home[:half] + low_from_x + low_from_y
    high_rows_out = home[half:] + high_from_x + high_from_y
    token_gradient = (
        input_base + jnp.concatenate([low_rows_out, high_rows_out], axis=0).astype(F32)
    ).astype(BF16)
    return (projected, token_gradient, down_grad, up_grad)


def solution(mesh):
    in_specs = (
        P("adapter", "fsdp"),
        P("adapter"),
        P("adapter", None, None),
        P("fsdp", None),
        P("adapter", "fsdp", None),
        P("adapter", None, "fsdp"),
        P("adapter", "fsdp"),
    )
    out_specs = (
        P("adapter", "fsdp"),
        P("adapter", "fsdp"),
        P("adapter", "fsdp", None),
        P("adapter", None, "fsdp"),
    )
    program = shards if mesh.shape["adapter"] == 8 and mesh.shape["fsdp"] == 4 else shards_any
    return jax.shard_map(program, mesh=mesh, in_specs=in_specs, out_specs=out_specs, check_vma=False)
```
